256 devices in a mesh: rows: 32 (over x, z_lo, y), dates: 8 (over z_hi, core).
Axes of the slice: x: 4, y: 4, z: 8 (z_hi: 4, z_lo: 2; z = z_hi * 2 + z_lo), core: 2. Of those that a mesh axis runs over, the one named last changes fastest.
Arguments:
- reflectance: float32 [32, 7, 1024, 1024], P('dates', None, 'rows'), may hold values from 0.05 to 0.9
- sun_zenith: float32 [32, 1024, 1024], P('dates', 'rows'), may hold values from 0.35 to 1
- view_zenith: float32 [32, 1024, 1024], P('dates', 'rows'), may hold values from 0 to 0.2
- rel_azimuth: float32 [32, 1024, 1024], P('dates', 'rows'), may hold values from -3.140625 to 3.140625
- flags: int32 [32, 1024, 1024], P('dates', 'rows'), may hold values from 0 to 3
- nadir_sun: float32 [1024, 1024], P('rows'), may hold values from 0.5 to 0.8
Outputs:
- normalized: float32 [32, 7, 1024, 1024], P('dates', None, 'rows')
The draws below stay inside these ranges and needn't reach their ends.
All inputs are finite; a program needn't handle non-finite values.
Results may differ from the reference program's by a relative error of at most 0.0003.
Values sent between devices are 32-bit elements; how exact they have to be, the bound alone decides.
No kernel may reach another device: no remote copies, remote signals or barrier semaphores. Data moves between devices by JAX's collectives and lax.ppermute only.
A program may use at most 128 MiB of HBM per device.

```python
import math
import jax
import jax.numpy as jnp
from jax import lax

ROWS_DEV = 32
COLS = 1024
BANDS = 7
HEIGHT = 1024
DATES = 32
N_ROWS = 32


def plant(values, stream_key, low, top_value):
    index_at = [jax.random.randint(jax.random.fold_in(stream_key, axis), (), 0, length) for axis, length in enumerate(values.shape)]
    longest = values.shape.index(max(values.shape))
    beside = index_at[:longest] + [(index_at[longest] + 1) % values.shape[longest]] + index_at[longest + 1:]
    return values.at[tuple(index_at)].set(low).at[tuple(beside)].set(top_value)


def levels(key, dims, cuts, low, top_value):
    def one(position, blocks):
        draws = jax.random.uniform(jax.random.fold_in(jax.random.fold_in(key, 6), position), (blocks,), jnp.float32, low / len(cuts), top_value / len(cuts))
        return jnp.repeat(jnp.exp(draws), dims[position] // blocks).reshape((-1,) + (1,) * (len(dims) - position - 1))

    level = one(*cuts[0])
    for cut in cuts[1:]:
        level = level * one(*cut)
    return level


def setup_inputs(seed: int = 0) -> dict:
    key_of = jax.random.split(jax.random.key(seed), 7)
    reflectance = jnp.clip(0.05 + 0.84999998 * jax.random.uniform(key_of[0], (DATES, BANDS, HEIGHT, COLS), jnp.float32) ** levels(key_of[0], (DATES, BANDS, HEIGHT, COLS), ((0, 8), (2, 32)), -0.2, 0.2), 0.05, 0.9)
    sun_zenith = jnp.clip(0.35 + 0.65 * jax.random.uniform(key_of[1], (DATES, HEIGHT, COLS), jnp.float32) ** levels(key_of[1], (DATES, HEIGHT, COLS), ((0, 8), (1, 32)), -0.2, 0.2), 0.35, 1.0)
    view_zenith = jnp.clip(0.2 * jax.random.uniform(key_of[2], (DATES, HEIGHT, COLS), jnp.float32) ** levels(key_of[2], (DATES, HEIGHT, COLS), ((0, 8), (1, 32)), -0.2, 0.2), 0.0, 0.2)
    rel_azimuth = jnp.clip(jax.random.uniform(key_of[3], (DATES, HEIGHT, COLS), jnp.float32, -3.140625, 3.140625), -3.140625, 3.140625)
    flags = plant(jax.random.randint(key_of[4], (DATES, HEIGHT, COLS), 0, 4), jax.random.fold_in(key_of[4], 1), 0, 3).astype(jnp.int32)
    nadir_sun = jnp.clip(0.5 + 0.3 * jax.random.uniform(key_of[5], (HEIGHT, COLS), jnp.float32) ** levels(key_of[5], (HEIGHT, COLS), ((0, 32),), -0.2, 0.2), 0.5, 0.8)
    return dict(reflectance=reflectance, sun_zenith=sun_zenith, view_zenith=view_zenith, rel_azimuth=rel_azimuth, flags=flags, nadir_sun=nadir_sun)


ridge_weight = 0.5
model_floor = 0.35

def ross_li(sun, view, azim):
    cos_sun = jnp.cos(sun)
    cos_view = jnp.cos(view)
    cos_phase = jnp.clip(cos_sun * cos_view + jnp.sin(sun) * jnp.sin(view) * jnp.cos(azim), -1.0, 1.0)
    phase_angle = jnp.arccos(cos_phase)
    kvol = ((0.5 * math.pi - phase_angle) * cos_phase + jnp.sin(phase_angle)) / (cos_sun + cos_view) - 0.25 * math.pi
    tan_sun = jnp.tan(sun)
    tan_view = jnp.tan(view)
    sec_sun = 1.0 / cos_sun
    sec_view = 1.0 / cos_view
    dist_sq = jnp.maximum(tan_sun * tan_sun + tan_view * tan_view - 2.0 * tan_sun * tan_view * jnp.cos(azim), 0.0)
    cross_term = tan_sun * tan_view * jnp.sin(azim)
    cos_shadow = jnp.clip(2.0 * jnp.sqrt(dist_sq + cross_term * cross_term) / (sec_sun + sec_view), -1.0, 1.0)
    shadow = jnp.arccos(cos_shadow)
    intersection = (shadow - jnp.sin(shadow) * cos_shadow) * (sec_sun + sec_view) / math.pi
    kgeo = intersection - sec_sun - sec_view + 0.5 * (1.0 + cos_phase) * sec_sun * sec_view
    return (kvol, kgeo)

def flag_weight(flags):
    return (0.3 * (flags == 1) + 0.7 * (flags == 2) + 1.0 * (flags == 3)).astype(jnp.float32)

def fit_params(refl, extras):
    kvol = extras[:, 0]
    kgeo = extras[:, 1]
    weight = extras[:, 2]
    n00 = lax.optimization_barrier(jnp.sum(weight, 0)) + ridge_weight
    n01 = lax.optimization_barrier(jnp.sum(weight * kvol, 0))
    n02 = lax.optimization_barrier(jnp.sum(weight * kgeo, 0))
    n11 = lax.optimization_barrier(jnp.sum(weight * kvol * kvol, 0)) + ridge_weight
    n12 = lax.optimization_barrier(jnp.sum(weight * kvol * kgeo, 0))
    n22 = lax.optimization_barrier(jnp.sum(weight * kgeo * kgeo, 0)) + ridge_weight
    weighted = weight[:, None] * refl
    rhs_iso = lax.optimization_barrier(jnp.sum(weighted, 0))
    rhs_vol = lax.optimization_barrier(jnp.sum(kvol[:, None] * weighted, 0))
    rhs_geo = lax.optimization_barrier(jnp.sum(kgeo[:, None] * weighted, 0))
    c00 = n11 * n22 - n12 * n12
    c01 = n02 * n12 - n01 * n22
    c02 = n01 * n12 - n02 * n11
    c11 = n00 * n22 - n02 * n02
    c12 = n01 * n02 - n00 * n12
    c22 = n00 * n11 - n01 * n01
    determ = n00 * c00 + n01 * c01 + n02 * c02
    inv_det = 1.0 / determ
    iso = (c00 * rhs_iso + c01 * rhs_vol + c02 * rhs_geo) * inv_det
    vol = (c01 * rhs_iso + c11 * rhs_vol + c12 * rhs_geo) * inv_det
    geo = (c02 * rhs_iso + c12 * rhs_vol + c22 * rhs_geo) * inv_det
    return jnp.stack([iso, vol, geo], 0)

def smooth_planes(padded, height, width):
    stencil = ((1.0, 2.0, 1.0), (2.0, 4.0, 2.0), (1.0, 2.0, 1.0))
    total = jnp.zeros(padded.shape[:2] + (height, width), jnp.float32)
    for row_off in range(3):
        for col_off in range(3):
            total = total + stencil[row_off][col_off] * padded[:, :, row_off:row_off + height, col_off:col_off + width]
    return total * (1.0 / 16.0)

def correct(refl, kvol, kgeo, smoothed, nadir_sun):
    kvol_nadir, kgeo_nadir = ross_li(nadir_sun, jnp.zeros_like(nadir_sun), jnp.zeros_like(nadir_sun))
    model_nadir = smoothed[0] + smoothed[1] * kvol_nadir[None] + smoothed[2] * kgeo_nadir[None]
    model_date = smoothed[0][None] + smoothed[1][None] * kvol[:, None] + smoothed[2][None] * kgeo[:, None]
    return refl * model_nadir[None] / jnp.maximum(model_date, model_floor)

def reference(reflectance, sun_zenith, view_zenith, rel_azimuth, flags, nadir_sun):

    def block_inputs(index):
        start = (index * ROWS_DEV).astype(jnp.int32)
        refl = lax.dynamic_slice_in_dim(reflectance, start, ROWS_DEV, 2)
        sun = lax.dynamic_slice_in_dim(sun_zenith, start, ROWS_DEV, 1)
        view = lax.dynamic_slice_in_dim(view_zenith, start, ROWS_DEV, 1)
        azim = lax.dynamic_slice_in_dim(rel_azimuth, start, ROWS_DEV, 1)
        flag_block = lax.dynamic_slice_in_dim(flags, start, ROWS_DEV, 1)
        kvol, kgeo = ross_li(sun, view, azim)
        return (refl, kvol, kgeo, flag_weight(flag_block), start)

    def block_fit(index):
        refl, kvol, kgeo, weight, start = block_inputs(index)
        return fit_params(refl, jnp.stack([kvol, kgeo, weight], 1))
    blocks = jnp.arange(N_ROWS, dtype=jnp.int32)
    params = lax.map(block_fit, blocks)
    params = params.transpose(1, 2, 0, 3, 4).reshape(3, BANDS, HEIGHT, COLS)
    padded = jnp.pad(params, ((0, 0), (0, 0), (1, 1), (1, 1)))
    smoothed = smooth_planes(padded, HEIGHT, COLS)

    def block_out(index):
        refl, kvol, kgeo, weight, start = block_inputs(index)
        smooth_block = lax.dynamic_slice_in_dim(smoothed, start, ROWS_DEV, 2)
        nadir_block = lax.dynamic_slice_in_dim(nadir_sun, start, ROWS_DEV, 0)
        return correct(refl, kvol, kgeo, smooth_block, nadir_block)
    outputs = lax.map(block_out, blocks)
    return outputs.transpose(1, 2, 0, 3, 4).reshape(DATES, BANDS, HEIGHT, COLS)
```

```python
import math

import jax
import jax.numpy as jnp
from jax import lax
from jax.experimental import pallas as pl
from jax.experimental.pallas import tpu as pltpu
from jax.sharding import PartitionSpec as P

ridge_weight = 0.5
model_floor = 0.35
LANES = 128
SUB = 8


SIN_SUN = (1.0, -0.1666666643, 0.008333314069, -0.0001983586641, 2.693759761e-06)
COS_SUN = (1.0, -0.4999999999, 0.04166666582, -0.001388885292, 2.479463838e-05, -2.693749222e-07)
SIN_VIEW = (1.0, -0.1666664847, 0.008321317392)
COS_VIEW = (1.0, -0.4999987263, 0.04158257081)
SIN_HALF = (1.0, -0.1666666662, 0.008333330977, -0.0001984086155, 2.752528678e-06, -2.388949223e-08)
GEO_POLY = (
    1.570796328, -1.214602072, -0.4109448018, 0.07413550608, -0.02841817795,
    0.01338202682, -0.005993092577, 0.001966222815, -0.0003219403671,
)
VOL_POLY = (
    0.999999995, -1.070795655, 0.08958698627, -0.02642109245, 0.01117480515,
    -0.004945099414, 0.001698688062, -0.0002986314728,
)


def poly(x, coefs):
    total = jnp.full_like(x, coefs[-1])
    for c in coefs[-2::-1]:
        total = total * x + c
    return total


def sin_cos_sun(sun):
    sq = sun * sun
    return sun * poly(sq, SIN_SUN), poly(sq, COS_SUN)


def shadow_term(cos_shadow):
    return jnp.sqrt(1.0 - cos_shadow) * poly(cos_shadow, GEO_POLY)


def ross_li(sun, view, azim):
    sin_s, cos_s = sin_cos_sun(sun)
    view_sq = view * view
    sin_v = view * poly(view_sq, SIN_VIEW)
    cos_v = poly(view_sq, COS_VIEW)
    half = 0.5 * azim
    sin_h = half * poly(half * half, SIN_HALF)
    half_sq = sin_h * sin_h
    cos_a = 1.0 - 2.0 * half_sq
    sin_a_sq = 4.0 * half_sq * (1.0 - half_sq)
    cos_cos = cos_s * cos_v
    sin_sin = sin_s * sin_v
    cos_phase = jnp.clip(cos_cos + sin_sin * cos_a, -1.0, 1.0)
    cos_sum = cos_s + cos_v
    inv = 1.0 / (cos_cos * cos_sum)
    sec_sec = cos_sum * inv
    inv_sum = cos_cos * inv
    kvol = (
        (0.5 * math.pi) * cos_phase + jnp.sqrt(1.0 - cos_phase) * poly(cos_phase, VOL_POLY)
    ) * inv_sum - 0.25 * math.pi
    tan_s = sin_s * cos_v
    tan_v = sin_v * cos_s
    dist_sq = jnp.maximum(tan_s * tan_s + tan_v * tan_v - 2.0 * tan_s * tan_v * cos_a, 0.0)
    cross_sq = sin_sin * sin_sin * sin_a_sq
    cos_shadow = jnp.clip(2.0 * jnp.sqrt(dist_sq + cross_sq) * inv_sum, -1.0, 1.0)
    kgeo = sec_sec * (
        cos_sum * (shadow_term(cos_shadow) * (1.0 / math.pi) - 1.0) + 0.5 * (1.0 + cos_phase)
    )
    return kvol, kgeo


def ross_li_nadir(sun):
    sin_s, cos_s = sin_cos_sun(sun)
    cos_sum = cos_s + 1.0
    inv = 1.0 / (cos_s * cos_sum)
    sec_s = cos_sum * inv
    inv_sum = cos_s * inv
    kvol = ((0.5 * math.pi - sun) * cos_s + sin_s) * inv_sum - 0.25 * math.pi
    cos_shadow = jnp.clip(2.0 * sin_s * inv_sum, -1.0, 1.0)
    kgeo = sec_s * (
        cos_sum * (shadow_term(cos_shadow) * (1.0 / math.pi) - 1.0) + 0.5 * (1.0 + cos_s)
    )
    return kvol, kgeo


def sums_kernel(blocks, refl, sun, view, azim, flags, *rest):
    del blocks
    sums, kernels = rest[-2:]
    dates, bands, rows, _ = refl.shape
    for g in range(rows // SUB):
        r = slice(g * SUB, (g + 1) * SUB)
        acc = [None] * (6 + 3 * bands)

        def add(i, x):
            acc[i] = x if acc[i] is None else acc[i] + x

        for t in range(dates):
            kvol, kgeo = ross_li(sun[t, r], view[t, r], azim[t, r])
            kernels[t, 0, r] = kvol
            kernels[t, 1, r] = kgeo
            f = flags[t, r]
            weight = jnp.where(f == 1, 0.3, jnp.where(f == 2, 0.7, jnp.where(f == 3, 1.0, 0.0)))
            weight = weight.astype(jnp.float32)
            wvol = weight * kvol
            wgeo = weight * kgeo
            for i, x in enumerate((weight, wvol, wgeo, wvol * kvol, wvol * kgeo, wgeo * kgeo)):
                add(i, x)
            for b in range(bands):
                x = refl[t, b, r]
                add(6 + b, weight * x)
                add(6 + bands + b, wvol * x)
                add(6 + 2 * bands + b, wgeo * x)
        for i, x in enumerate(acc):
            sums[0, i, r] = x


def date_sums(blocks, refl, sun, view, azim, flags, kernels=None):
    dates, bands, rows, cols = refl.shape
    parts = blocks.shape[0]
    planes = 6 + 3 * bands
    pixel = pl.BlockSpec((dates, rows, LANES), lambda i, b: (0, 0, b[i]))
    in_specs = [pl.BlockSpec((dates, bands, rows, LANES), lambda i, b: (0, 0, 0, b[i]))] + [pixel] * 4
    args = [blocks, refl, sun, view, azim, flags]
    aliases = {}
    if kernels is not None:
        in_specs.append(pl.BlockSpec(memory_space=pl.ANY))
        args.append(kernels)
        aliases = {6: 1}
    return pl.pallas_call(
        sums_kernel,
        grid_spec=pltpu.PrefetchScalarGridSpec(
            num_scalar_prefetch=1,
            grid=(parts,),
            in_specs=in_specs,
            out_specs=[
                pl.BlockSpec((1, planes, rows, LANES), lambda i, b: (i, 0, 0, 0)),
                pl.BlockSpec((dates, 2, rows, LANES), lambda i, b: (0, 0, 0, b[i])),
            ],
        ),
        out_shape=[
            jax.ShapeDtypeStruct((parts, planes, rows, LANES), jnp.float32),
            jax.ShapeDtypeStruct((dates, 2, rows, cols), jnp.float32),
        ],
        input_output_aliases=aliases,
        name="date_sums",
    )(*args)


def solve_kernel(own_a, own_b, near_lo, near_hi, far_lo, far_hi, params, edge_lo, edge_hi):
    planes, rows, _ = params.shape
    bands = planes // 3
    half = rows // 2
    for g in range(rows // SUB):
        r = slice(g * SUB, (g + 1) * SUB)
        low = g * SUB < half
        near, far = (near_lo, far_lo) if low else (near_hi, far_hi)
        start = g * SUB - (0 if low else half)
        q = slice(start, start + SUB)

        def total(i):
            return (own_a[0, i, r] + own_b[0, i, r]) + (near[i, q] + far[i, q])

        n00 = total(0) + ridge_weight
        n01 = total(1)
        n02 = total(2)
        n11 = total(3) + ridge_weight
        n12 = total(4)
        n22 = total(5) + ridge_weight
        c00 = n11 * n22 - n12 * n12
        c01 = n02 * n12 - n01 * n22
        c02 = n01 * n12 - n02 * n11
        c11 = n00 * n22 - n02 * n02
        c12 = n01 * n02 - n00 * n12
        c22 = n00 * n11 - n01 * n01
        inv_det = 1.0 / (n00 * c00 + n01 * c01 + n02 * c02)
        for b in range(bands):
            x, y, z = total(6 + b), total(6 + bands + b), total(6 + 2 * bands + b)
            values = (
                (c00 * x + c01 * y + c02 * z) * inv_det,
                (c01 * x + c11 * y + c12 * z) * inv_det,
                (c02 * x + c12 * y + c22 * z) * inv_det,
            )
            for k, v in enumerate(values):
                p = k * bands + b
                params[p, r] = v
                if g == 0:
                    edge_lo[p : p + 1] = v[:1]
                if g == rows // SUB - 1:
                    edge_hi[p : p + 1] = v[SUB - 1 :]


def solve(own_a, own_b, near_lo, near_hi, far_lo, far_hi, bands):
    rows = own_a.shape[2]
    full = lambda x: pl.BlockSpec(x.shape, lambda i, n=len(x.shape): (0,) * n)
    one = pl.BlockSpec((1,) + own_a.shape[1:], lambda i: (0, 0, 0, 0))
    edge = jax.ShapeDtypeStruct((3 * bands, LANES), jnp.float32)
    outs = [jax.ShapeDtypeStruct((3 * bands, rows, LANES), jnp.float32), edge, edge]
    return pl.pallas_call(
        solve_kernel,
        grid=(1,),
        in_specs=[one, one] + [full(x) for x in (near_lo, near_hi, far_lo, far_hi)],
        out_specs=[full(x) for x in outs],
        out_shape=outs,
        name="solve",
    )(own_a, own_b, near_lo, near_hi, far_lo, far_hi)


def rows_kernel(params, above, below, low, high):
    planes, rows, _ = params.shape
    half = rows // 2
    for p in range(planes):
        x = params[p]
        up = jnp.concatenate([above[p : p + 1], x[:-1]], 0)
        down = jnp.concatenate([x[1:], below[p : p + 1]], 0)
        y = (up + 2.0 * x + down) * 0.25
        low[p] = y[:half]
        high[p] = y[half:]


def smooth_rows(params, above, below):
    planes, rows, _ = params.shape
    out = jax.ShapeDtypeStruct((planes, rows // 2, LANES), jnp.float32)
    return pl.pallas_call(rows_kernel, out_shape=[out, out], name="smooth_rows")(params, above, below)


def correct_kernel(places, refl, kernels, nadir, *rest):
    pieces, (out, strip) = rest[:-2], rest[-2:]
    step = pl.program_id(0)
    parts = pl.num_programs(0)
    dates, bands, rows, _ = refl.shape
    half = rows // 2

    @pl.when(step == 0)
    def _():
        strip[0] = jnp.zeros(strip.shape[1:], jnp.float32)
        strip[parts + 1] = jnp.zeros(strip.shape[1:], jnp.float32)
        for i in range(0, len(pieces), 2):
            place = places[i // 2] + 1
            strip[place, :, :half] = pieces[i][...]
            strip[place, :, half:] = pieces[i + 1][...]

    lane = lax.broadcasted_iota(jnp.int32, (SUB, LANES), 1)
    first, last = lane == 0, lane == LANES - 1
    for g in range(rows // SUB):
        r = slice(g * SUB, (g + 1) * SUB)
        kvol_n, kgeo_n = ross_li_nadir(nadir[r])

        def smooth(p):
            x = strip[step + 1, p, r]
            prior = jnp.where(first, pltpu.roll(strip[step, p, r], 1, 1), pltpu.roll(x, 1, 1))
            later = jnp.where(
                last,
                pltpu.roll(strip[step + 2, p, r], LANES - 1, 1),
                pltpu.roll(x, LANES - 1, 1),
            )
            return (prior + 2.0 * x + later) * 0.25

        for b in range(bands):
            iso, vol, geo = smooth(b), smooth(bands + b), smooth(2 * bands + b)
            model_n = iso + vol * kvol_n + geo * kgeo_n
            for t in range(dates):
                model = iso + vol * kernels[t, 0, r] + geo * kernels[t, 1, r]
                out[t, b, r] = refl[t, b, r] * model_n / jnp.maximum(model, model_floor)


def correct(places, refl, kernels, nadir, pieces):
    dates, bands, rows, cols = refl.shape
    parts = cols // LANES
    whole = pl.BlockSpec(pieces[0].shape, lambda i, p: (0, 0, 0))
    cube = pl.BlockSpec((dates, bands, rows, LANES), lambda i, p: (0, 0, 0, i))
    return pl.pallas_call(
        correct_kernel,
        grid_spec=pltpu.PrefetchScalarGridSpec(
            num_scalar_prefetch=1,
            grid=(parts,),
            in_specs=[
                cube,
                pl.BlockSpec((dates, 2, rows, LANES), lambda i, p: (0, 0, 0, i)),
                pl.BlockSpec((rows, LANES), lambda i, p: (0, i)),
            ]
            + [whole] * len(pieces),
            out_specs=cube,
            scratch_shapes=[pltpu.VMEM((parts + 2, 3 * bands, rows, LANES), jnp.float32)],
        ),
        out_shape=jax.ShapeDtypeStruct(refl.shape, jnp.float32),
        name="correct",
    )(places, refl, kernels, nadir, *pieces)


def per_device(reflectance, sun_zenith, view_zenith, rel_azimuth, flags, nadir_sun):
    devices = lax.axis_size("dates")
    ring = devices // 2
    index = lax.axis_index("dates")
    place, core = index // 2, index % 2
    bands, rows = reflectance.shape[1:3]
    half = rows // 2

    def shift(x, by):
        return lax.ppermute(x, "dates", [(i, (i + 2 * by) % devices) for i in range(devices)])

    def swap(x):
        return lax.ppermute(x, "dates", [(i, i ^ 1) for i in range(devices)])

    ahead = (place + jnp.arange(ring, dtype=jnp.int32)) % ring
    inputs = (reflectance, sun_zenith, view_zenith, rel_azimuth, flags)
    other, kernels = date_sums((1 - core) * ring + ahead, *inputs)
    other = swap(other)
    mine, kernels = date_sums(core * ring + ahead, *inputs, kernels)

    def both(part, low):
        cut = slice(0, half) if low else slice(half, rows)
        return mine[part, :, cut] + other[part, :, cut]

    far_up = shift(both(2, True), 1)
    far_dn = shift(both(2, False), -1)
    near_up = shift(both(1, False), 1)
    near_dn = shift(both(3, True), -1)
    sum_up = shift(both(1, True) + far_up, 1)
    sum_dn = shift(both(3, False) + far_dn, -1)
    params, edge_lo, edge_hi = solve(mine, other, sum_up, sum_dn, near_dn, near_up, bands)

    blocks = lax.axis_size("rows")
    above = lax.ppermute(edge_hi, "rows", [(i, i + 1) for i in range(blocks - 1)])
    below = lax.ppermute(edge_lo, "rows", [(i + 1, i) for i in range(blocks - 1)])
    low, high = smooth_rows(params, above, below)

    low_up = shift(low, 1)
    high_dn = shift(high, -1)
    high_up = shift(high, 1)
    low_dn = shift(low, -1)
    low_far = shift(low_up, 1)
    high_far = shift(high_dn, -1)
    pieces = (low, high, low_up, high_up, low_far, high_far, low_dn, high_dn)
    pieces = pieces + tuple(swap(x) for x in pieces)
    behind = (place - jnp.arange(ring, dtype=jnp.int32)) % ring
    places = jnp.concatenate([core * ring + behind, (1 - core) * ring + behind])
    return correct(places, reflectance, kernels, nadir_sun, pieces)


def solution(mesh):
    in_specs = (
        P("dates", None, "rows", None),
        P("dates", "rows", None),
        P("dates", "rows", None),
        P("dates", "rows", None),
        P("dates", "rows", None),
        P("rows", None),
    )
    out_specs = P("dates", None, "rows", None)
    return jax.shard_map(
        per_device, mesh=mesh, in_specs=in_specs, out_specs=out_specs, check_vma=False
    )
```

```python
import math

import jax
import jax.numpy as jnp
from jax import lax
from jax.experimental import pallas as pl
from jax.experimental.pallas import tpu as pltpu
from jax.sharding import PartitionSpec as P

ridge_weight = 0.5
model_floor = 0.35
LANES = 128
SUB = 8
VMEM = pl.BlockSpec(memory_space=pltpu.VMEM)


SIN_SUN = (1.0, -0.1666666643, 0.008333314069, -0.0001983586641, 2.693759761e-06)
COS_SUN = (1.0, -0.4999999999, 0.04166666582, -0.001388885292, 2.479463838e-05, -2.693749222e-07)
SIN_VIEW = (1.0, -0.1666664847, 0.008321317392)
COS_VIEW = (1.0, -0.4999987263, 0.04158257081)
SIN_HALF = (1.0, -0.1666666662, 0.008333330977, -0.0001984086155, 2.752528678e-06, -2.388949223e-08)
GEO_POLY = (
    1.570796328, -1.214602072, -0.4109448018, 0.07413550608, -0.02841817795,
    0.01338202682, -0.005993092577, 0.001966222815, -0.0003219403671,
)
VOL_POLY = (
    0.999999995, -1.070795655, 0.08958698627, -0.02642109245, 0.01117480515,
    -0.004945099414, 0.001698688062, -0.0002986314728,
)


def poly(x, coefs):
    total = jnp.full_like(x, coefs[-1])
    for c in coefs[-2::-1]:
        total = total * x + c
    return total


def sin_cos_sun(sun):
    sq = sun * sun
    return sun * poly(sq, SIN_SUN), poly(sq, COS_SUN)


def shadow_term(cos_shadow):
    return jnp.sqrt(1.0 - cos_shadow) * poly(cos_shadow, GEO_POLY)


def ross_li(sun, view, azim):
    sin_s, cos_s = sin_cos_sun(sun)
    view_sq = view * view
    sin_v = view * poly(view_sq, SIN_VIEW)
    cos_v = poly(view_sq, COS_VIEW)
    half = 0.5 * azim
    sin_h = half * poly(half * half, SIN_HALF)
    half_sq = sin_h * sin_h
    cos_a = 1.0 - 2.0 * half_sq
    sin_a_sq = 4.0 * half_sq * (1.0 - half_sq)
    cos_cos = cos_s * cos_v
    sin_sin = sin_s * sin_v
    cos_phase = jnp.clip(cos_cos + sin_sin * cos_a, -1.0, 1.0)
    cos_sum = cos_s + cos_v
    inv = 1.0 / (cos_cos * cos_sum)
    sec_sec = cos_sum * inv
    inv_sum = cos_cos * inv
    kvol = (
        (0.5 * math.pi) * cos_phase + jnp.sqrt(1.0 - cos_phase) * poly(cos_phase, VOL_POLY)
    ) * inv_sum - 0.25 * math.pi
    tan_s = sin_s * cos_v
    tan_v = sin_v * cos_s
    dist_sq = jnp.maximum(tan_s * tan_s + tan_v * tan_v - 2.0 * tan_s * tan_v * cos_a, 0.0)
    cross_sq = sin_sin * sin_sin * sin_a_sq
    cos_shadow = jnp.clip(2.0 * jnp.sqrt(dist_sq + cross_sq) * inv_sum, -1.0, 1.0)
    kgeo = sec_sec * (
        cos_sum * (shadow_term(cos_shadow) * (1.0 / math.pi) - 1.0) + 0.5 * (1.0 + cos_phase)
    )
    return kvol, kgeo


def ross_li_nadir(sun):
    sin_s, cos_s = sin_cos_sun(sun)
    cos_sum = cos_s + 1.0
    inv = 1.0 / (cos_s * cos_sum)
    sec_s = cos_sum * inv
    inv_sum = cos_s * inv
    kvol = ((0.5 * math.pi - sun) * cos_s + sin_s) * inv_sum - 0.25 * math.pi
    cos_shadow = jnp.clip(2.0 * sin_s * inv_sum, -1.0, 1.0)
    kgeo = sec_s * (
        cos_sum * (shadow_term(cos_shadow) * (1.0 / math.pi) - 1.0) + 0.5 * (1.0 + cos_s)
    )
    return kvol, kgeo


def part_of(rel, core_flip, ring):
    index = lax.axis_index("dates")
    core = lax.rem(index, 2)
    core = 1 - core if core_flip else core
    return core * ring + lax.rem(lax.div(index, 2) + rel, ring)


def lanes_of(part):
    return pl.ds(pl.multiple_of(part * LANES, LANES), LANES)


def weight_of(f):
    weight = jnp.where(f == 1, 0.3, jnp.where(f == 2, 0.7, jnp.where(f == 3, 1.0, 0.0)))
    return weight.astype(jnp.float32)


def add_dates(sums, part, block, refl, flags, kernel_of):
    dates, bands, rows, _ = refl.shape
    lanes = lanes_of(block)
    for g in range(rows // SUB):
        r = slice(g * SUB, (g + 1) * SUB)
        acc = [None] * (6 + 3 * bands)

        def add(i, x):
            acc[i] = x if acc[i] is None else acc[i] + x

        for t in range(dates):
            kvol, kgeo = kernel_of(t, r)
            weight = weight_of(flags[t, r, lanes])
            wvol = weight * kvol
            wgeo = weight * kgeo
            for i, x in enumerate((weight, wvol, wgeo, wvol * kvol, wvol * kgeo, wgeo * kgeo)):
                add(i, x)
            for b in range(bands):
                x = refl[t, b, r, lanes]
                add(6 + b, weight * x)
                add(6 + bands + b, wvol * x)
                add(6 + 2 * bands + b, wgeo * x)
        for i, x in enumerate(acc):
            sums[part, i, r] = x


def other_kernel(*refs):
    sources, (sums, kernels), held, sems = refs[:5], refs[5:7], refs[7:12], refs[12]
    refl, sun, view, azim, flags = held
    dates, _, rows, cols = refl.shape
    ring = sums.shape[0]
    copies = [
        [pltpu.make_async_copy(sources[k].at[t], held[k].at[t], sems.at[k, t]) for t in range(dates)]
        for k in range(5)
    ]
    for t in range(dates):
        for k in range(1, 5):
            copies[k][t].start()
    for t in range(dates):
        copies[0][t].start()
    for t in range(dates):
        for k in range(1, 4):
            copies[k][t].wait()

        def angles(i, carry):
            block = part_of(i, True, ring)
            lanes = lanes_of(block)
            for g in range(rows // SUB):
                r = slice(g * SUB, (g + 1) * SUB)
                kvol, kgeo = ross_li(sun[t, r, lanes], view[t, r, lanes], azim[t, r, lanes])
                kernels[block, t, 0, r] = kvol
                kernels[block, t, 1, r] = kgeo
            return carry

        lax.fori_loop(0, ring, angles, 0)
    for t in range(dates):
        copies[4][t].wait()
        copies[0][t].wait()

    def one(i, carry):
        block = part_of(i, True, ring)
        add_dates(sums, i, block, refl, flags, lambda t, r: (kernels[block, t, 0, r], kernels[block, t, 1, r]))
        return carry

    lax.fori_loop(0, ring, one, 0)


def own_kernel(refl, sun, view, azim, flags, _, sums, kernels):
    ring = sums.shape[0]

    def one(i, carry):
        block = part_of(i, False, ring)
        lanes = lanes_of(block)

        def kernel_of(t, r):
            kvol, kgeo = ross_li(sun[t, r, lanes], view[t, r, lanes], azim[t, r, lanes])
            kernels[block, t, 0, r] = kvol
            kernels[block, t, 1, r] = kgeo
            return kvol, kgeo

        add_dates(sums, i, block, refl, flags, kernel_of)
        return carry

    lax.fori_loop(0, ring, one, 0)


def sums_shapes(refl):
    dates, bands, rows, cols = refl.shape
    parts = cols // LANES
    return [
        jax.ShapeDtypeStruct((parts // 2, 6 + 3 * bands, rows, LANES), jnp.float32),
        jax.ShapeDtypeStruct((parts, dates, 2, rows, LANES), jnp.float32),
    ]


def other_sums(*inputs):
    held = [jax.ShapeDtypeStruct(x.shape, x.dtype) for x in inputs]
    return pl.pallas_call(
        other_kernel,
        in_specs=[pl.BlockSpec(memory_space=pltpu.HBM)] * 5,
        out_specs=[VMEM] * 7,
        out_shape=sums_shapes(inputs[0]) + held,
        scratch_shapes=[pltpu.SemaphoreType.DMA((5, inputs[0].shape[0]))],
        compiler_params=pltpu.CompilerParams(vmem_limit_bytes=16 << 20),
        name="other_sums",
    )(*(pltpu.with_memory_space_constraint(x, pltpu.HBM) for x in inputs))


def own_sums(inputs, kernels):
    return pl.pallas_call(
        own_kernel,
        in_specs=[VMEM] * 6,
        out_specs=[VMEM] * 2,
        out_shape=sums_shapes(inputs[0]),
        input_output_aliases={5: 1},
        compiler_params=pltpu.CompilerParams(vmem_limit_bytes=16 << 20),
        name="own_sums",
    )(*inputs, kernels)


def solve_kernel(own_a, own_b, near_lo, near_hi, far_lo, far_hi, low, high, whole, edge_lo, edge_hi):
    planes, rows, _ = whole.shape
    bands = planes // 3
    half = rows // 2
    groups = rows // SUB
    for g in range(groups):
        r = slice(g * SUB, (g + 1) * SUB)
        near, far = (near_lo, far_lo) if g < groups // 2 else (near_hi, far_hi)
        start = g * SUB % half
        q = slice(start, start + SUB)

        def total(i):
            return (own_a[0, i, r] + own_b[0, i, r]) + (near[i, q] + far[i, q])

        n00 = total(0) + ridge_weight
        n01 = total(1)
        n02 = total(2)
        n11 = total(3) + ridge_weight
        n12 = total(4)
        n22 = total(5) + ridge_weight
        c00 = n11 * n22 - n12 * n12
        c01 = n02 * n12 - n01 * n22
        c02 = n01 * n12 - n02 * n11
        c11 = n00 * n22 - n02 * n02
        c12 = n01 * n02 - n00 * n12
        c22 = n00 * n11 - n01 * n01
        inv_det = 1.0 / (n00 * c00 + n01 * c01 + n02 * c02)
        for b in range(bands):
            x, y, z = total(6 + b), total(6 + bands + b), total(6 + 2 * bands + b)
            whole[b, r] = (c00 * x + c01 * y + c02 * z) * inv_det
            whole[bands + b, r] = (c01 * x + c11 * y + c12 * z) * inv_det
            whole[2 * bands + b, r] = (c02 * x + c12 * y + c22 * z) * inv_det
    row = lax.broadcasted_iota(jnp.int32, (SUB, LANES), 0)
    first, last = row == 0, row == SUB - 1
    zero = jnp.zeros((SUB, LANES), jnp.float32)
    for p in range(planes):
        x = [whole[p, g * SUB : (g + 1) * SUB] for g in range(groups)]
        edge_lo[p : p + 1] = x[0][:1]
        edge_hi[p : p + 1] = x[-1][SUB - 1 :]
        for g in range(groups):
            prior = jnp.where(last, x[g - 1] if g else zero, x[g])
            later = jnp.where(first, x[g + 1] if g < groups - 1 else zero, x[g])
            y = (pltpu.roll(prior, 1, 0) + 2.0 * x[g] + pltpu.roll(later, SUB - 1, 0)) * 0.25
            whole[p, g * SUB : (g + 1) * SUB] = y
            start = g * SUB % half
            (low if g < groups // 2 else high)[p, start : start + SUB] = y


def solve(own_a, own_b, near_lo, near_hi, far_lo, far_hi, bands):
    rows = own_a.shape[2]
    shape = lambda *dims: jax.ShapeDtypeStruct(dims, jnp.float32)
    piece, edge = shape(3 * bands, rows // 2, LANES), shape(3 * bands, LANES)
    return pl.pallas_call(
        solve_kernel,
        in_specs=[VMEM] * 6,
        out_specs=[VMEM] * 5,
        out_shape=[piece, piece, shape(3 * bands, rows, LANES), edge, edge],
        compiler_params=pltpu.CompilerParams(vmem_limit_bytes=16 << 20),
        name="solve",
    )(own_a, own_b, near_lo, near_hi, far_lo, far_hi)


def correct_kernel(refl, kernels, nadir, halo_a, halo_b, *rest):
    pieces, (out, strip) = rest[:-2], rest[-2:]
    step = pl.program_id(0)
    parts = pl.num_programs(0)
    dates, bands, rows, _ = out.shape
    planes = 3 * bands
    half = rows // 2
    each = halo_a.shape[0]

    @pl.when(step == 0)
    def _():
        strip[0] = jnp.zeros(strip.shape[1:], jnp.float32)
        strip[parts + 1] = jnp.zeros(strip.shape[1:], jnp.float32)
        count = 0
        for k in range(2 * each):
            place = part_of((each - k % each) % each, k >= each, each) + 1
            top = 0
            while top < rows:
                piece = pieces[count]
                strip[place, :, top : top + piece.shape[1]] = piece[...]
                top += piece.shape[1]
                count += 1
            halo = (halo_a if k < each else halo_b)[k % each]
            for p in range(planes):
                strip[place, p, :1] += 0.25 * halo[p : p + 1]
                strip[place, p, rows - 1 :] += 0.25 * halo[planes + p : planes + p + 1]

    lanes = lanes_of(step)
    lane = lax.broadcasted_iota(jnp.int32, (SUB, LANES), 1)
    first, last = lane == 0, lane == LANES - 1
    for g in range(rows // SUB):
        r = slice(g * SUB, (g + 1) * SUB)
        kvol_n, kgeo_n = ross_li_nadir(nadir[r, lanes])

        def smooth(p):
            x = strip[step + 1, p, r]
            prior = pltpu.roll(jnp.where(last, strip[step, p, r], x), 1, 1)
            later = pltpu.roll(jnp.where(first, strip[step + 2, p, r], x), LANES - 1, 1)
            return (prior + 2.0 * x + later) * 0.25

        for b in range(bands):
            iso, vol, geo = smooth(b), smooth(bands + b), smooth(2 * bands + b)
            model_n = iso + vol * kvol_n + geo * kgeo_n
            for t in range(dates):
                model = iso + vol * kernels[step, t, 0, r] + geo * kernels[step, t, 1, r]
                out[t, b, r] = refl[t, b, r, lanes] * model_n / jnp.maximum(model, model_floor)


def correct(refl, kernels, nadir, halo_a, halo_b, pieces):
    dates, bands, rows, cols = refl.shape
    parts = cols // LANES
    return pl.pallas_call(
        correct_kernel,
        grid=(parts,),
        in_specs=[VMEM] * (5 + len(pieces)),
        out_specs=pl.BlockSpec((dates, bands, rows, LANES), lambda i: (0, 0, 0, i)),
        scratch_shapes=[pltpu.VMEM((parts + 2, 3 * bands, rows, LANES), jnp.float32)],
        out_shape=jax.ShapeDtypeStruct(refl.shape, jnp.float32),
        compiler_params=pltpu.CompilerParams(vmem_limit_bytes=24 << 20),
        name="correct",
    )(refl, kernels, nadir, halo_a, halo_b, *pieces)


def per_device(reflectance, sun_zenith, view_zenith, rel_azimuth, flags, nadir_sun):
    devices = lax.axis_size("dates")
    bands, rows = reflectance.shape[1:3]
    half = rows // 2

    def shift(x, by):
        return lax.ppermute(x, "dates", [(i, (i + 2 * by) % devices) for i in range(devices)])

    def swap(x):
        return lax.ppermute(x, "dates", [(i, i ^ 1) for i in range(devices)])

    other, kernels, *held = other_sums(reflectance, sun_zenith, view_zenith, rel_azimuth, flags)
    other = swap(other)
    mine, kernels = own_sums(held, kernels)

    def both(part, low):
        cut = slice(0, half) if low else slice(half, rows)
        return mine[part, :, cut] + other[part, :, cut]

    far_up = shift(both(2, True), 1)
    far_dn = shift(both(2, False), -1)
    near_up = shift(both(1, False), 1)
    near_dn = shift(both(3, True), -1)
    sum_up = shift(both(1, True) + far_up, 1)
    sum_dn = shift(both(3, False) + far_dn, -1)
    low, high, whole, edge_lo, edge_hi = solve(mine, other, sum_up, sum_dn, near_dn, near_up, bands)

    low_up = shift(low, 1)
    high_dn = shift(high, -1)
    high_up = shift(high, 1)
    low_dn = shift(low, -1)
    low_far = shift(low_up, 1)
    high_far = shift(high_dn, -1)
    others = (low_up, high_up, low_far, high_far, low_dn, high_dn)
    pieces = (low, high) + others + tuple(swap(x) for x in (whole,) + others)

    blocks = lax.axis_size("rows")
    above = lax.ppermute(edge_hi, "rows", [(i, i + 1) for i in range(blocks - 1)])
    below = lax.ppermute(edge_lo, "rows", [(i + 1, i) for i in range(blocks - 1)])
    halo = jnp.concatenate([above, below], 0)
    halo = jnp.stack([halo, shift(halo, 1), shift(halo, 2), shift(halo, -1)])
    return correct(held[0], kernels, nadir_sun, halo, swap(halo), pieces)


def solution(mesh):
    in_specs = (
        P("dates", None, "rows", None),
        P("dates", "rows", None),
        P("dates", "rows", None),
        P("dates", "rows", None),
        P("dates", "rows", None),
        P("rows", None),
    )
    out_specs = P("dates", None, "rows", None)
    return jax.shard_map(
        per_device, mesh=mesh, in_specs=in_specs, out_specs=out_specs, check_vma=False
    )
```

```python
import math

import jax
import jax.numpy as jnp
from jax import lax
from jax.experimental import pallas as pl
from jax.experimental.pallas import tpu as pltpu
from jax.sharding import PartitionSpec as P

ridge_weight = 0.5
model_floor = 0.35
LANES = 128
SUB = 8
VMEM = pl.BlockSpec(memory_space=pltpu.VMEM)


SIN_SUN = (1.0, -0.1666666643, 0.008333314069, -0.0001983586641, 2.693759761e-06)
COS_SUN = (1.0, -0.4999999999, 0.04166666582, -0.001388885292, 2.479463838e-05, -2.693749222e-07)
SIN_VIEW = (1.0, -0.1666664847, 0.008321317392)
COS_VIEW = (1.0, -0.4999987263, 0.04158257081)
SIN_HALF = (1.0, -0.1666666662, 0.008333330977, -0.0001984086155, 2.752528678e-06, -2.388949223e-08)
GEO_POLY = (
    1.570796328, -1.214602072, -0.4109448018, 0.07413550608, -0.02841817795,
    0.01338202682, -0.005993092577, 0.001966222815, -0.0003219403671,
)
VOL_POLY = (
    0.999999995, -1.070795655, 0.08958698627, -0.02642109245, 0.01117480515,
    -0.004945099414, 0.001698688062, -0.0002986314728,
)


def poly(x, coefs):
    total = jnp.full_like(x, coefs[-1])
    for c in coefs[-2::-1]:
        total = total * x + c
    return total


def sin_cos_sun(sun):
    sq = sun * sun
    return sun * poly(sq, SIN_SUN), poly(sq, COS_SUN)


def shadow_term(cos_shadow):
    return jnp.sqrt(1.0 - cos_shadow) * poly(cos_shadow, GEO_POLY)


def ross_li(sun, view, azim):
    sin_s, cos_s = sin_cos_sun(sun)
    view_sq = view * view
    sin_v = view * poly(view_sq, SIN_VIEW)
    cos_v = poly(view_sq, COS_VIEW)
    half = 0.5 * azim
    sin_h = half * poly(half * half, SIN_HALF)
    half_sq = sin_h * sin_h
    cos_a = 1.0 - 2.0 * half_sq
    sin_a_sq = 4.0 * half_sq * (1.0 - half_sq)
    cos_cos = cos_s * cos_v
    sin_sin = sin_s * sin_v
    cos_phase = jnp.clip(cos_cos + sin_sin * cos_a, -1.0, 1.0)
    cos_sum = cos_s + cos_v
    inv = 1.0 / (cos_cos * cos_sum)
    sec_sec = cos_sum * inv
    inv_sum = cos_cos * inv
    kvol = (
        (0.5 * math.pi) * cos_phase + jnp.sqrt(1.0 - cos_phase) * poly(cos_phase, VOL_POLY)
    ) * inv_sum - 0.25 * math.pi
    tan_s = sin_s * cos_v
    tan_v = sin_v * cos_s
    dist_sq = jnp.maximum(tan_s * tan_s + tan_v * tan_v - 2.0 * tan_s * tan_v * cos_a, 0.0)
    cross_sq = sin_sin * sin_sin * sin_a_sq
    cos_shadow = jnp.clip(2.0 * jnp.sqrt(dist_sq + cross_sq) * inv_sum, -1.0, 1.0)
    kgeo = sec_sec * (
        cos_sum * (shadow_term(cos_shadow) * (1.0 / math.pi) - 1.0) + 0.5 * (1.0 + cos_phase)
    )
    return kvol, kgeo


def ross_li_nadir(sun):
    sin_s, cos_s = sin_cos_sun(sun)
    cos_sum = cos_s + 1.0
    inv = 1.0 / (cos_s * cos_sum)
    sec_s = cos_sum * inv
    inv_sum = cos_s * inv
    kvol = ((0.5 * math.pi - sun) * cos_s + sin_s) * inv_sum - 0.25 * math.pi
    cos_shadow = jnp.clip(2.0 * sin_s * inv_sum, -1.0, 1.0)
    kgeo = sec_s * (
        cos_sum * (shadow_term(cos_shadow) * (1.0 / math.pi) - 1.0) + 0.5 * (1.0 + cos_s)
    )
    return kvol, kgeo


def ring_place():
    index = lax.axis_index("dates")
    core = lax.rem(index, 2)
    return lax.div(index, 2), core, 1 - 2 * core


def part_at(place, core, ring):
    return core * ring + lax.rem(place + 2 * ring, ring)


def sums_part(i, flip, ring):
    place, core, way = ring_place()
    if flip:
        core, way = 1 - core, -way
    by = jnp.where(i == 0, 0, jnp.where(i == 3, 2, way))
    return part_at(place + by, jnp.where(i == 2, 1 - core, core), ring)


def lanes_of(part):
    return pl.ds(pl.multiple_of(part * LANES, LANES), LANES)


def weight_of(f):
    weight = jnp.where(f == 1, 0.3, jnp.where(f == 2, 0.7, jnp.where(f == 3, 1.0, 0.0)))
    return weight.astype(jnp.float32)


def spot(g):
    return (0, 2, 3, 1)[g]


def add_dates(sums, part, block, refl, flags, kernel_of):
    dates, bands, rows, _ = refl.shape
    lanes = lanes_of(block)
    for g in range(rows // SUB):
        r = slice(g * SUB, (g + 1) * SUB)
        acc = [None] * (6 + 3 * bands)

        def add(i, x):
            acc[i] = x if acc[i] is None else acc[i] + x

        for t in range(dates):
            kvol, kgeo = kernel_of(t, r)
            weight = weight_of(flags[t, r, lanes])
            wvol = weight * kvol
            wgeo = weight * kgeo
            for i, x in enumerate((weight, wvol, wgeo, wvol * kvol, wvol * kgeo, wgeo * kgeo)):
                add(i, x)
            for b in range(bands):
                x = refl[t, b, r, lanes]
                add(6 + b, weight * x)
                add(6 + bands + b, wvol * x)
                add(6 + 2 * bands + b, wgeo * x)
        q = slice(spot(g) * SUB, (spot(g) + 1) * SUB)
        for i, x in enumerate(acc):
            sums[part, i, q] = x


def other_kernel(*refs):
    sources, (sums, kernels), held, sems = refs[:5], refs[5:7], refs[7:12], refs[12]
    refl, sun, view, azim, flags = held
    dates, _, rows, _ = refl.shape
    ring = sums.shape[0]
    copies = [
        [pltpu.make_async_copy(sources[k].at[t], held[k].at[t], sems.at[k, t]) for t in range(dates)]
        for k in range(5)
    ]
    for t in range(dates):
        for k in range(1, 5):
            copies[k][t].start()
    for t in range(dates):
        copies[0][t].start()
    for t in range(dates):
        for k in range(1, 4):
            copies[k][t].wait()

        def angles(i, carry):
            block = sums_part(i, True, ring)
            lanes = lanes_of(block)
            for g in range(rows // SUB):
                r = slice(g * SUB, (g + 1) * SUB)
                kvol, kgeo = ross_li(sun[t, r, lanes], view[t, r, lanes], azim[t, r, lanes])
                kernels[block, t, 0, r] = kvol
                kernels[block, t, 1, r] = kgeo
            return carry

        lax.fori_loop(0, ring, angles, 0)
    for t in range(dates):
        copies[4][t].wait()
        copies[0][t].wait()

    def one(i, carry):
        block = sums_part(i, True, ring)
        add_dates(sums, i, block, refl, flags, lambda t, r: (kernels[block, t, 0, r], kernels[block, t, 1, r]))
        return carry

    lax.fori_loop(0, ring, one, 0)


def own_kernel(refl, sun, view, azim, flags, _, sums, kernels):
    ring = sums.shape[0]

    def one(i, carry):
        block = sums_part(i, False, ring)
        lanes = lanes_of(block)

        def kernel_of(t, r):
            kvol, kgeo = ross_li(sun[t, r, lanes], view[t, r, lanes], azim[t, r, lanes])
            kernels[block, t, 0, r] = kvol
            kernels[block, t, 1, r] = kgeo
            return kvol, kgeo

        add_dates(sums, i, block, refl, flags, kernel_of)
        return carry

    lax.fori_loop(0, ring, one, 0)


def sums_shapes(refl):
    dates, bands, rows, cols = refl.shape
    parts = cols // LANES
    return [
        jax.ShapeDtypeStruct((parts // 2, 6 + 3 * bands, rows, LANES), jnp.float32),
        jax.ShapeDtypeStruct((parts, dates, 2, rows, LANES), jnp.float32),
    ]


def other_sums(*inputs):
    held = [jax.ShapeDtypeStruct(x.shape, x.dtype) for x in inputs]
    return pl.pallas_call(
        other_kernel,
        in_specs=[pl.BlockSpec(memory_space=pltpu.HBM)] * 5,
        out_specs=[VMEM] * 7,
        out_shape=sums_shapes(inputs[0]) + held,
        scratch_shapes=[pltpu.SemaphoreType.DMA((5, inputs[0].shape[0]))],
        compiler_params=pltpu.CompilerParams(vmem_limit_bytes=16 << 20),
        name="other_sums",
    )(*(pltpu.with_memory_space_constraint(x, pltpu.HBM) for x in inputs))


def own_sums(inputs, kernels):
    return pl.pallas_call(
        own_kernel,
        in_specs=[VMEM] * 6,
        out_specs=[VMEM] * 2,
        out_shape=sums_shapes(inputs[0]),
        input_output_aliases={5: 1},
        compiler_params=pltpu.CompilerParams(vmem_limit_bytes=16 << 20),
        name="own_sums",
    )(*inputs, kernels)


def solve_group(own_a, own_b, near, far, bands, g, store):
    r = slice(spot(g) * SUB, (spot(g) + 1) * SUB)
    start = spot(g) % 2 * SUB
    q = slice(start, start + SUB)

    def total(i):
        return (own_a[0, i, r] + own_b[0, i, r]) + (near[i, r] + far[i, q])

    n00 = total(0) + ridge_weight
    n01 = total(1)
    n02 = total(2)
    n11 = total(3) + ridge_weight
    n12 = total(4)
    n22 = total(5) + ridge_weight
    c00 = n11 * n22 - n12 * n12
    c01 = n02 * n12 - n01 * n22
    c02 = n01 * n12 - n02 * n11
    c11 = n00 * n22 - n02 * n02
    c12 = n01 * n02 - n00 * n12
    c22 = n00 * n11 - n01 * n01
    inv_det = 1.0 / (n00 * c00 + n01 * c01 + n02 * c02)
    for b in range(bands):
        x, y, z = total(6 + b), total(6 + bands + b), total(6 + 2 * bands + b)
        store(b, q, (c00 * x + c01 * y + c02 * z) * inv_det)
        store(bands + b, q, (c01 * x + c11 * y + c12 * z) * inv_det)
        store(2 * bands + b, q, (c02 * x + c12 * y + c22 * z) * inv_det)


def edges_kernel(own_a, own_b, near, far, edges, first, last):
    planes = edges.shape[0]

    def store(p, q, x):
        edges[p, q] = x

    for g in (0, 3):
        solve_group(own_a, own_b, near, far, planes // 3, g, store)
    for p in range(planes):
        first[p : p + 1] = edges[p, :1]
        last[p : p + 1] = edges[p, 2 * SUB - 1 :]


def middle_kernel(own_a, own_b, near, far, edges, above, below, smooth, middle):
    planes, rows, _ = smooth.shape

    def store(p, q, x):
        middle[p, q] = x

    for g in (1, 2):
        solve_group(own_a, own_b, near, far, planes // 3, g, store)
    row = lax.broadcasted_iota(jnp.int32, (SUB, LANES), 0)
    first, last = row == 0, row == SUB - 1
    wide = lambda x: jnp.broadcast_to(x, (SUB, LANES))
    for p in range(planes):
        x = [
            wide(above[p : p + 1]),
            edges[p, :SUB],
            middle[p, :SUB],
            middle[p, SUB:],
            edges[p, SUB:],
            wide(below[p : p + 1]),
        ]
        for g in range(rows // SUB):
            here = x[g + 1]
            prior = pltpu.roll(jnp.where(last, x[g], here), 1, 0)
            later = pltpu.roll(jnp.where(first, x[g + 2], here), SUB - 1, 0)
            smooth[p, g * SUB : (g + 1) * SUB] = (prior + 2.0 * here + later) * 0.25


def solve_edges(own_a, own_b, near, far, bands):
    shape = lambda *dims: jax.ShapeDtypeStruct(dims, jnp.float32)
    return pl.pallas_call(
        edges_kernel,
        in_specs=[VMEM] * 4,
        out_specs=[VMEM] * 3,
        out_shape=[shape(3 * bands, 2 * SUB, LANES)] + [shape(3 * bands, LANES)] * 2,
        compiler_params=pltpu.CompilerParams(vmem_limit_bytes=16 << 20),
        name="solve_edges",
    )(own_a, own_b, near, far)


def solve_middle(own_a, own_b, near, far, edges, above, below):
    rows = own_a.shape[2]
    return pl.pallas_call(
        middle_kernel,
        in_specs=[VMEM] * 7,
        out_specs=VMEM,
        out_shape=jax.ShapeDtypeStruct((edges.shape[0], rows, LANES), jnp.float32),
        scratch_shapes=[pltpu.VMEM(edges.shape, jnp.float32)],
        compiler_params=pltpu.CompilerParams(vmem_limit_bytes=16 << 20),
        name="solve_middle",
    )(own_a, own_b, near, far, edges, above, below)


def correct_kernel(refl, kernels, nadir, *rest):
    pieces, (out, strip) = rest[:-2], rest[-2:]
    step = pl.program_id(0)
    parts = pl.num_programs(0)
    dates, bands, rows, _ = out.shape
    ring = len(pieces) // 2

    @pl.when(step == 0)
    def _():
        strip[0] = jnp.zeros(strip.shape[1:], jnp.float32)
        strip[parts + 1] = jnp.zeros(strip.shape[1:], jnp.float32)
        place, core, way = ring_place()
        spots = [(0, 0), (-way, 0), (-way, 1), (-2 * way, 0)]
        spots += [(0, 1), (way, 1), (way, 0), (2 * way, 1)]
        for (by, flip), piece in zip(spots, pieces):
            strip[part_at(place + by, 1 - core if flip else core, ring) + 1] = piece[...]

    lanes = lanes_of(step)
    lane = lax.broadcasted_iota(jnp.int32, (SUB, LANES), 1)
    first, last = lane == 0, lane == LANES - 1
    for g in range(rows // SUB):
        r = slice(g * SUB, (g + 1) * SUB)
        kvol_n, kgeo_n = ross_li_nadir(nadir[r, lanes])

        def smooth(p):
            x = strip[step + 1, p, r]
            prior = pltpu.roll(jnp.where(last, strip[step, p, r], x), 1, 1)
            later = pltpu.roll(jnp.where(first, strip[step + 2, p, r], x), LANES - 1, 1)
            return (prior + 2.0 * x + later) * 0.25

        for b in range(bands):
            iso, vol, geo = smooth(b), smooth(bands + b), smooth(2 * bands + b)
            model_n = iso + vol * kvol_n + geo * kgeo_n
            for t in range(dates):
                model = iso + vol * kernels[step, t, 0, r] + geo * kernels[step, t, 1, r]
                out[t, b, r] = refl[t, b, r, lanes] * model_n / jnp.maximum(model, model_floor)


def correct(refl, kernels, nadir, pieces):
    dates, bands, rows, cols = refl.shape
    parts = cols // LANES
    return pl.pallas_call(
        correct_kernel,
        grid=(parts,),
        in_specs=[VMEM] * (3 + len(pieces)),
        out_specs=pl.BlockSpec((dates, bands, rows, LANES), lambda i: (0, 0, 0, i)),
        scratch_shapes=[pltpu.VMEM((parts + 2, 3 * bands, rows, LANES), jnp.float32)],
        out_shape=jax.ShapeDtypeStruct(refl.shape, jnp.float32),
        compiler_params=pltpu.CompilerParams(vmem_limit_bytes=24 << 20),
        name="correct",
    )(refl, kernels, nadir, *pieces)


def per_device(reflectance, sun_zenith, view_zenith, rel_azimuth, flags, nadir_sun):
    devices = lax.axis_size("dates")
    bands, rows = reflectance.shape[1:3]
    half = rows // 2

    def onward(x):
        pairs = [(i, (i + 2 - 4 * (i % 2)) % devices) for i in range(devices)]
        return lax.ppermute(x, "dates", pairs)

    def swap(x):
        return lax.ppermute(x, "dates", [(i, i ^ 1) for i in range(devices)])

    other, kernels, *held = other_sums(reflectance, sun_zenith, view_zenith, rel_azimuth, flags)
    other = swap(other)
    mine, kernels = own_sums(held, kernels)
    far = onward(mine[3] + other[3])
    near = onward(mine[2] + other[2])
    edge_sums = onward(mine[1, :, :half] + other[1, :, :half] + far[:, :half])
    middle_sums = onward(mine[1, :, half:] + other[1, :, half:] + far[:, half:])
    near = swap(near)
    edges, first, last = solve_edges(mine, other, near, edge_sums, bands)
    blocks = lax.axis_size("rows")
    above = lax.ppermute(last, "rows", [(i, i + 1) for i in range(blocks - 1)])
    below = lax.ppermute(first, "rows", [(i + 1, i) for i in range(blocks - 1)])
    own = solve_middle(mine, other, near, middle_sums, edges, above, below)

    behind = onward(own)
    partner = swap(own)
    behind_partner = onward(partner)
    relayed = onward(behind)
    pieces = (own, behind, behind_partner, relayed, partner)
    pieces += (swap(behind), swap(behind_partner), swap(relayed))
    return correct(held[0], kernels, nadir_sun, pieces)


def solution(mesh):
    in_specs = (
        P("dates", None, "rows", None),
        P("dates", "rows", None),
        P("dates", "rows", None),
        P("dates", "rows", None),
        P("dates", "rows", None),
        P("rows", None),
    )
    out_specs = P("dates", None, "rows", None)

    return jax.shard_map(
        per_device, mesh=mesh, in_specs=in_specs, out_specs=out_specs, check_vma=False
    )
```

```python
import math

import jax
import jax.numpy as jnp
from jax import lax
from jax.experimental import pallas as pl
from jax.experimental.pallas import tpu as pltpu
from jax.sharding import PartitionSpec as P

ridge_weight = 0.5
model_floor = 0.35
LANES = 128
SUB = 8
VMEM = pl.BlockSpec(memory_space=pltpu.VMEM)


SIN_SUN = (1.0, -0.1666666643, 0.008333314069, -0.0001983586641, 2.693759761e-06)
COS_SUN = (1.0, -0.4999999999, 0.04166666582, -0.001388885292, 2.479463838e-05, -2.693749222e-07)
SIN_VIEW = (1.0, -0.1666664847, 0.008321317392)
COS_VIEW = (1.0, -0.4999987263, 0.04158257081)
SIN_HALF = (1.0, -0.1666666662, 0.008333330977, -0.0001984086155, 2.752528678e-06, -2.388949223e-08)
GEO_POLY = (
    1.570796328, -1.214602072, -0.4109448018, 0.07413550608, -0.02841817795,
    0.01338202682, -0.005993092577, 0.001966222815, -0.0003219403671,
)
VOL_POLY = (
    0.999999995, -1.070795655, 0.08958698627, -0.02642109245, 0.01117480515,
    -0.004945099414, 0.001698688062, -0.0002986314728,
)


def poly(x, coefs):
    total = jnp.full_like(x, coefs[-1])
    for c in coefs[-2::-1]:
        total = total * x + c
    return total


def sin_cos_sun(sun):
    sq = sun * sun
    return sun * poly(sq, SIN_SUN), poly(sq, COS_SUN)


def shadow_term(cos_shadow):
    return jnp.sqrt(1.0 - cos_shadow) * poly(cos_shadow, GEO_POLY)


def ross_li(sun, view, azim):
    sin_s, cos_s = sin_cos_sun(sun)
    view_sq = view * view
    sin_v = view * poly(view_sq, SIN_VIEW)
    cos_v = poly(view_sq, COS_VIEW)
    half = 0.5 * azim
    sin_h = half * poly(half * half, SIN_HALF)
    half_sq = sin_h * sin_h
    cos_a = 1.0 - 2.0 * half_sq
    sin_a_sq = 4.0 * half_sq * (1.0 - half_sq)
    cos_cos = cos_s * cos_v
    sin_sin = sin_s * sin_v
    cos_phase = jnp.clip(cos_cos + sin_sin * cos_a, -1.0, 1.0)
    cos_sum = cos_s + cos_v
    inv = 1.0 / (cos_cos * cos_sum)
    sec_sec = cos_sum * inv
    inv_sum = cos_cos * inv
    kvol = (
        (0.5 * math.pi) * cos_phase + jnp.sqrt(1.0 - cos_phase) * poly(cos_phase, VOL_POLY)
    ) * inv_sum - 0.25 * math.pi
    tan_s = sin_s * cos_v
    tan_v = sin_v * cos_s
    dist_sq = jnp.maximum(tan_s * tan_s + tan_v * tan_v - 2.0 * tan_s * tan_v * cos_a, 0.0)
    cross_sq = sin_sin * sin_sin * sin_a_sq
    cos_shadow = jnp.clip(2.0 * jnp.sqrt(dist_sq + cross_sq) * inv_sum, -1.0, 1.0)
    kgeo = sec_sec * (
        cos_sum * (shadow_term(cos_shadow) * (1.0 / math.pi) - 1.0) + 0.5 * (1.0 + cos_phase)
    )
    return kvol, kgeo


def ross_li_nadir(sun):
    sin_s, cos_s = sin_cos_sun(sun)
    cos_sum = cos_s + 1.0
    inv = 1.0 / (cos_s * cos_sum)
    sec_s = cos_sum * inv
    inv_sum = cos_s * inv
    kvol = ((0.5 * math.pi - sun) * cos_s + sin_s) * inv_sum - 0.25 * math.pi
    cos_shadow = jnp.clip(2.0 * sin_s * inv_sum, -1.0, 1.0)
    kgeo = sec_s * (
        cos_sum * (shadow_term(cos_shadow) * (1.0 / math.pi) - 1.0) + 0.5 * (1.0 + cos_s)
    )
    return kvol, kgeo


def ring_place():
    index = lax.axis_index("dates")
    core = lax.rem(index, 2)
    return lax.div(index, 2), core, 1 - 2 * core


def part_at(place, core, ring):
    return core * ring + lax.rem(place + 2 * ring, ring)


def sums_part(i, flip, ring):
    place, core, way = ring_place()
    if flip:
        core, way = 1 - core, -way
    by = jnp.where(i == 0, 0, jnp.where(i == 3, 2, way))
    return part_at(place + by, jnp.where(i == 2, 1 - core, core), ring)


def lanes_of(part):
    return pl.ds(pl.multiple_of(part * LANES, LANES), LANES)


def weight_of(f):
    weight = jnp.where(f == 1, 0.3, jnp.where(f == 2, 0.7, jnp.where(f == 3, 1.0, 0.0)))
    return weight.astype(jnp.float32)


def add_dates(sums, part, block, refl, flags, kernel_of):
    dates, bands, rows, _ = refl.shape
    lanes = lanes_of(block)
    for g in range(rows // SUB):
        r = slice(g * SUB, (g + 1) * SUB)
        acc = [None] * (6 + 3 * bands)

        def add(i, x):
            acc[i] = x if acc[i] is None else acc[i] + x

        for t in range(dates):
            kvol, kgeo = kernel_of(t, r)
            weight = weight_of(flags[t, r, lanes])
            wvol = weight * kvol
            wgeo = weight * kgeo
            for i, x in enumerate((weight, wvol, wgeo, wvol * kvol, wvol * kgeo, wgeo * kgeo)):
                add(i, x)
            for b in range(bands):
                x = refl[t, b, r, lanes]
                add(6 + b, weight * x)
                add(6 + bands + b, wvol * x)
                add(6 + 2 * bands + b, wgeo * x)
        for i, x in enumerate(acc):
            sums[part, i, r] = x


def other_kernel(*refs):
    sources, (sums, kernels), held, sems = refs[:5], refs[5:7], refs[7:12], refs[12]
    refl, sun, view, azim, flags = held
    dates, _, rows, _ = refl.shape
    ring = sums.shape[0]
    copies = [
        [pltpu.make_async_copy(sources[k].at[t], held[k].at[t], sems.at[k, t]) for t in range(dates)]
        for k in range(5)
    ]
    for t in range(dates):
        for k in range(1, 5):
            copies[k][t].start()
    for t in range(dates):
        copies[0][t].start()
    for t in range(dates):
        for k in range(1, 4):
            copies[k][t].wait()

        def angles(i, carry):
            block = sums_part(i, True, ring)
            lanes = lanes_of(block)
            for g in range(rows // SUB):
                r = slice(g * SUB, (g + 1) * SUB)
                kvol, kgeo = ross_li(sun[t, r, lanes], view[t, r, lanes], azim[t, r, lanes])
                kernels[block, t, 0, r] = kvol
                kernels[block, t, 1, r] = kgeo
            return carry

        lax.fori_loop(0, ring, angles, 0)
    for t in range(dates):
        copies[4][t].wait()
        copies[0][t].wait()

    def one(i, carry):
        block = sums_part(i, True, ring)
        add_dates(sums, i, block, refl, flags, lambda t, r: (kernels[block, t, 0, r], kernels[block, t, 1, r]))
        return carry

    lax.fori_loop(0, ring, one, 0)


def own_kernel(refl, sun, view, azim, flags, _, sums, kernels):
    ring = sums.shape[0]

    def one(i, carry):
        block = sums_part(i, False, ring)
        lanes = lanes_of(block)

        def kernel_of(t, r):
            kvol, kgeo = ross_li(sun[t, r, lanes], view[t, r, lanes], azim[t, r, lanes])
            kernels[block, t, 0, r] = kvol
            kernels[block, t, 1, r] = kgeo
            return kvol, kgeo

        add_dates(sums, i, block, refl, flags, kernel_of)
        return carry

    lax.fori_loop(0, ring, one, 0)


def sums_shapes(refl):
    dates, bands, rows, cols = refl.shape
    parts = cols // LANES
    return [
        jax.ShapeDtypeStruct((parts // 2, 6 + 3 * bands, rows, LANES), jnp.float32),
        jax.ShapeDtypeStruct((parts, dates, 2, rows, LANES), jnp.float32),
    ]


def other_sums(*inputs):
    held = [jax.ShapeDtypeStruct(x.shape, x.dtype) for x in inputs]
    return pl.pallas_call(
        other_kernel,
        in_specs=[pl.BlockSpec(memory_space=pltpu.HBM)] * 5,
        out_specs=[VMEM] * 7,
        out_shape=sums_shapes(inputs[0]) + held,
        scratch_shapes=[pltpu.SemaphoreType.DMA((5, inputs[0].shape[0]))],
        compiler_params=pltpu.CompilerParams(vmem_limit_bytes=16 << 20),
        name="other_sums",
    )(*(pltpu.with_memory_space_constraint(x, pltpu.HBM) for x in inputs))


def own_sums(inputs, kernels):
    return pl.pallas_call(
        own_kernel,
        in_specs=[VMEM] * 6,
        out_specs=[VMEM] * 2,
        out_shape=sums_shapes(inputs[0]),
        input_output_aliases={5: 1},
        compiler_params=pltpu.CompilerParams(vmem_limit_bytes=16 << 20),
        name="own_sums",
    )(*inputs, kernels)


def solve_kernel(own_a, own_b, near, far, smooth, above, below):
    planes, rows, _ = smooth.shape
    bands = planes // 3
    groups = rows // SUB
    for g in range(groups):
        r = slice(g * SUB, (g + 1) * SUB)

        def total(i):
            return (own_a[0, i, r] + own_b[0, i, r]) + (near[i, r] + far[i, r])

        n00 = total(0) + ridge_weight
        n01 = total(1)
        n02 = total(2)
        n11 = total(3) + ridge_weight
        n12 = total(4)
        n22 = total(5) + ridge_weight
        c00 = n11 * n22 - n12 * n12
        c01 = n02 * n12 - n01 * n22
        c02 = n01 * n12 - n02 * n11
        c11 = n00 * n22 - n02 * n02
        c12 = n01 * n02 - n00 * n12
        c22 = n00 * n11 - n01 * n01
        inv_det = 1.0 / (n00 * c00 + n01 * c01 + n02 * c02)
        for b in range(bands):
            x, y, z = total(6 + b), total(6 + bands + b), total(6 + 2 * bands + b)
            smooth[b, r] = (c00 * x + c01 * y + c02 * z) * inv_det
            smooth[bands + b, r] = (c01 * x + c11 * y + c12 * z) * inv_det
            smooth[2 * bands + b, r] = (c02 * x + c12 * y + c22 * z) * inv_det
    row = lax.broadcasted_iota(jnp.int32, (SUB, LANES), 0)
    first, last = row == 0, row == SUB - 1
    zero = jnp.zeros((SUB, LANES), jnp.float32)
    above[...] = jnp.zeros(above.shape, jnp.float32)
    below[...] = jnp.zeros(below.shape, jnp.float32)
    for p in range(planes):
        x = [smooth[p, g * SUB : (g + 1) * SUB] for g in range(groups)]
        below[0, p : p + 1] = x[0][:1] * 0.25
        above[0, p : p + 1] = x[-1][SUB - 1 :] * 0.25
        for g in range(groups):
            prior = jnp.where(last, x[g - 1] if g else zero, x[g])
            later = jnp.where(first, x[g + 1] if g < groups - 1 else zero, x[g])
            y = (pltpu.roll(prior, 1, 0) + 2.0 * x[g] + pltpu.roll(later, SUB - 1, 0)) * 0.25
            smooth[p, g * SUB : (g + 1) * SUB] = y


def solve(own_a, own_b, near, far, bands):
    rows = own_a.shape[2]
    shape = lambda *dims: jax.ShapeDtypeStruct(dims, jnp.float32)
    return pl.pallas_call(
        solve_kernel,
        in_specs=[VMEM] * 4,
        out_specs=[VMEM] * 3,
        out_shape=[shape(3 * bands, rows, LANES)] + [shape(1, rows, LANES)] * 2,
        compiler_params=pltpu.CompilerParams(vmem_limit_bytes=16 << 20),
        name="solve",
    )(own_a, own_b, near, far)


def correct_kernel(refl, kernels, nadir, above, below, *rest):
    (own, partner, near_a, far_a, end_a, near_b, far_b, end_b), (out, strip) = rest[:-2], rest[-2:]
    step = pl.program_id(0)
    parts = pl.num_programs(0)
    dates, bands, rows, _ = out.shape
    planes, ring = 3 * bands, parts // 2

    @pl.when(step == 0)
    def _():
        strip[0] = jnp.zeros(strip.shape[1:], jnp.float32)
        strip[parts + 1] = jnp.zeros(strip.shape[1:], jnp.float32)
        place, core, way = ring_place()
        halo = lambda ref, at: (ref.at[at], ref.at[at + 1])
        for by, flip, piece, (top, bottom) in (
            (0, 0, own, (above.at[0], below.at[0])),
            (0, 1, partner, halo(partner, planes)),
            (-way, 0, near_a, halo(far_a, planes + 2)),
            (-way, 1, far_a, halo(far_a, planes)),
            (-2 * way, 1, end_a, halo(end_a, planes)),
            (way, 1, near_b, halo(far_b, planes + 2)),
            (way, 0, far_b, halo(far_b, planes)),
            (2 * way, 0, end_b, halo(end_b, planes)),
        ):
            spot = part_at(place + by, 1 - core if flip else core, ring) + 1
            for p in range(planes):
                strip[spot, p] = piece[p]
                strip[spot, p, :1] += top[p : p + 1]
                strip[spot, p, rows - 1 :] += bottom[p : p + 1]

    lanes = lanes_of(step)
    lane = lax.broadcasted_iota(jnp.int32, (SUB, LANES), 1)
    first, last = lane == 0, lane == LANES - 1
    for g in range(rows // SUB):
        r = slice(g * SUB, (g + 1) * SUB)
        kvol_n, kgeo_n = ross_li_nadir(nadir[r, lanes])

        def smooth(p):
            x = strip[step + 1, p, r]
            prior = pltpu.roll(jnp.where(last, strip[step, p, r], x), 1, 1)
            later = pltpu.roll(jnp.where(first, strip[step + 2, p, r], x), LANES - 1, 1)
            return (prior + 2.0 * x + later) * 0.25

        for b in range(bands):
            iso, vol, geo = smooth(b), smooth(bands + b), smooth(2 * bands + b)
            model_n = iso + vol * kvol_n + geo * kgeo_n
            for t in range(dates):
                model = iso + vol * kernels[step, t, 0, r] + geo * kernels[step, t, 1, r]
                out[t, b, r] = refl[t, b, r, lanes] * model_n / jnp.maximum(model, model_floor)


def correct(refl, kernels, nadir, *pieces):
    dates, bands, rows, cols = refl.shape
    parts = cols // LANES
    return pl.pallas_call(
        correct_kernel,
        grid=(parts,),
        in_specs=[VMEM] * (3 + len(pieces)),
        out_specs=pl.BlockSpec((dates, bands, rows, LANES), lambda i: (0, 0, 0, i)),
        scratch_shapes=[pltpu.VMEM((parts + 2, 3 * bands, rows, LANES), jnp.float32)],
        out_shape=jax.ShapeDtypeStruct(refl.shape, jnp.float32),
        compiler_params=pltpu.CompilerParams(vmem_limit_bytes=24 << 20),
        name="correct",
    )(refl, kernels, nadir, *pieces)


def per_device(reflectance, sun_zenith, view_zenith, rel_azimuth, flags, nadir_sun):
    devices = lax.axis_size("dates")
    bands = reflectance.shape[1]

    def onward(x):
        pairs = [(i, (i + 2 - 4 * (i % 2)) % devices) for i in range(devices)]
        return lax.ppermute(x, "dates", pairs)

    def swap(x):
        return lax.ppermute(x, "dates", [(i, i ^ 1) for i in range(devices)])

    other, kernels, *held = other_sums(reflectance, sun_zenith, view_zenith, rel_azimuth, flags)
    other = swap(other)
    mine, kernels = own_sums(held, kernels)
    far = onward(mine[3] + other[3])
    near = onward(mine[2] + other[2])
    far = onward(mine[1] + other[1] + far)
    near = swap(near)
    own, above, below = solve(mine, other, near, far, bands)

    near = onward(own)
    blocks = lax.axis_size("rows")
    above = lax.ppermute(above, "rows", [(i, i + 1) for i in range(blocks - 1)])
    below = lax.ppermute(below, "rows", [(i + 1, i) for i in range(blocks - 1)])
    partner = swap(jnp.concatenate([own, above, below], 0))
    far = onward(jnp.concatenate([partner, above, below], 0))
    end = onward(far[: 3 * bands + 2])
    pieces = (own, partner, near, far, end)
    pieces += (swap(near), swap(far), swap(end))
    return correct(held[0], kernels, nadir_sun, above, below, *pieces)


def solution(mesh):
    in_specs = (
        P("dates", None, "rows", None),
        P("dates", "rows", None),
        P("dates", "rows", None),
        P("dates", "rows", None),
        P("dates", "rows", None),
        P("rows", None),
    )
    out_specs = P("dates", None, "rows", None)

    return jax.shard_map(
        per_device, mesh=mesh, in_specs=in_specs, out_specs=out_specs, check_vma=False
    )
```

```python
import math

import jax
import jax.numpy as jnp
from jax import lax
from jax.experimental import pallas as pl
from jax.experimental.pallas import tpu as pltpu
from jax.sharding import PartitionSpec as P

ridge_weight = 0.5
model_floor = 0.35
LANES = 128
SUB = 8
VMEM = pl.BlockSpec(memory_space=pltpu.VMEM)


SIN_SUN = (1.0, -0.1666666643, 0.008333314069, -0.0001983586641, 2.693759761e-06)
COS_SUN = (1.0, -0.4999999999, 0.04166666582, -0.001388885292, 2.479463838e-05, -2.693749222e-07)
SIN_VIEW = (1.0, -0.1666664847, 0.008321317392)
COS_VIEW = (1.0, -0.4999987263, 0.04158257081)
SIN_HALF = (1.0, -0.1666666662, 0.008333330977, -0.0001984086155, 2.752528678e-06, -2.388949223e-08)
GEO_POLY = (
    1.570796328, -1.214602072, -0.4109448018, 0.07413550608, -0.02841817795,
    0.01338202682, -0.005993092577, 0.001966222815, -0.0003219403671,
)
VOL_POLY = (
    0.999999995, -1.070795655, 0.08958698627, -0.02642109245, 0.01117480515,
    -0.004945099414, 0.001698688062, -0.0002986314728,
)


def poly(x, coefs):
    total = jnp.full_like(x, coefs[-1])
    for c in coefs[-2::-1]:
        total = total * x + c
    return total


def sin_cos_sun(sun):
    sq = sun * sun
    return sun * poly(sq, SIN_SUN), poly(sq, COS_SUN)


def shadow_term(cos_shadow):
    return jnp.sqrt(1.0 - cos_shadow) * poly(cos_shadow, GEO_POLY)


def ross_li(sun, view, azim):
    sin_s, cos_s = sin_cos_sun(sun)
    view_sq = view * view
    sin_v = view * poly(view_sq, SIN_VIEW)
    cos_v = poly(view_sq, COS_VIEW)
    half = 0.5 * azim
    sin_h = half * poly(half * half, SIN_HALF)
    half_sq = sin_h * sin_h
    cos_a = 1.0 - 2.0 * half_sq
    sin_a_sq = 4.0 * half_sq * (1.0 - half_sq)
    cos_cos = cos_s * cos_v
    sin_sin = sin_s * sin_v
    cos_phase = jnp.clip(cos_cos + sin_sin * cos_a, -1.0, 1.0)
    cos_sum = cos_s + cos_v
    inv = 1.0 / (cos_cos * cos_sum)
    sec_sec = cos_sum * inv
    inv_sum = cos_cos * inv
    kvol = (
        (0.5 * math.pi) * cos_phase + jnp.sqrt(1.0 - cos_phase) * poly(cos_phase, VOL_POLY)
    ) * inv_sum - 0.25 * math.pi
    tan_s = sin_s * cos_v
    tan_v = sin_v * cos_s
    dist_sq = jnp.maximum(tan_s * tan_s + tan_v * tan_v - 2.0 * tan_s * tan_v * cos_a, 0.0)
    cross_sq = sin_sin * sin_sin * sin_a_sq
    cos_shadow = jnp.clip(2.0 * jnp.sqrt(dist_sq + cross_sq) * inv_sum, -1.0, 1.0)
    kgeo = sec_sec * (
        cos_sum * (shadow_term(cos_shadow) * (1.0 / math.pi) - 1.0) + 0.5 * (1.0 + cos_phase)
    )
    return kvol, kgeo


def ross_li_nadir(sun):
    sin_s, cos_s = sin_cos_sun(sun)
    cos_sum = cos_s + 1.0
    inv = 1.0 / (cos_s * cos_sum)
    sec_s = cos_sum * inv
    inv_sum = cos_s * inv
    kvol = ((0.5 * math.pi - sun) * cos_s + sin_s) * inv_sum - 0.25 * math.pi
    cos_shadow = jnp.clip(2.0 * sin_s * inv_sum, -1.0, 1.0)
    kgeo = sec_s * (
        cos_sum * (shadow_term(cos_shadow) * (1.0 / math.pi) - 1.0) + 0.5 * (1.0 + cos_s)
    )
    return kvol, kgeo


def ring_place():
    index = lax.axis_index("dates")
    core = lax.rem(index, 2)
    return lax.div(index, 2), core, 1 - 2 * core


def part_at(place, core, ring):
    return core * ring + lax.rem(place + 2 * ring, ring)


def sums_part(i, flip, ring):
    place, core, way = ring_place()
    if flip:
        core, way = 1 - core, -way
    by = jnp.where(i == 0, 0, jnp.where(i == 3, 2, way))
    return part_at(place + by, jnp.where(i == 2, 1 - core, core), ring)


def lanes_of(part):
    return pl.ds(pl.multiple_of(part * LANES, LANES), LANES)


def weight_of(f):
    weight = jnp.where(f == 1, 0.3, jnp.where(f == 2, 0.7, jnp.where(f == 3, 1.0, 0.0)))
    return weight.astype(jnp.float32)


def add_dates(sums, part, block, refl, flags, kernel_of):
    dates, bands, rows, _ = refl.shape
    lanes = lanes_of(block)
    for g in range(rows // SUB):
        r = slice(g * SUB, (g + 1) * SUB)
        acc = [None] * (6 + 3 * bands)

        def add(i, x):
            acc[i] = x if acc[i] is None else acc[i] + x

        for t in range(dates):
            kvol, kgeo = kernel_of(t, r)
            weight = weight_of(flags[t, r, lanes])
            wvol = weight * kvol
            wgeo = weight * kgeo
            for i, x in enumerate((weight, wvol, wgeo, wvol * kvol, wvol * kgeo, wgeo * kgeo)):
                add(i, x)
            for b in range(bands):
                x = refl[t, b, r, lanes]
                add(6 + b, weight * x)
                add(6 + bands + b, wvol * x)
                add(6 + 2 * bands + b, wgeo * x)
        for i, x in enumerate(acc):
            sums[part, i, r] = x


def other_kernel(*refs):
    sources, (sums, kernels), held, sems = refs[:5], refs[5:7], refs[7:12], refs[12]
    refl, sun, view, azim, flags = held
    dates, _, rows, _ = refl.shape
    ring = sums.shape[0]
    copies = [
        [pltpu.make_async_copy(sources[k].at[t], held[k].at[t], sems.at[k, t]) for t in range(dates)]
        for k in range(5)
    ]
    for t in range(dates):
        for k in range(1, 5):
            copies[k][t].start()
    for t in range(dates):
        copies[0][t].start()
    for t in range(dates):
        for k in range(1, 4):
            copies[k][t].wait()

        def angles(i, carry):
            block = sums_part(i, True, ring)
            lanes = lanes_of(block)
            for g in range(rows // SUB):
                r = slice(g * SUB, (g + 1) * SUB)
                kvol, kgeo = ross_li(sun[t, r, lanes], view[t, r, lanes], azim[t, r, lanes])
                kernels[block, t, 0, r] = kvol
                kernels[block, t, 1, r] = kgeo
            return carry

        lax.fori_loop(0, ring, angles, 0)
    for t in range(dates):
        copies[4][t].wait()
        copies[0][t].wait()

    def one(i, carry):
        block = sums_part(i, True, ring)
        add_dates(sums, i, block, refl, flags, lambda t, r: (kernels[block, t, 0, r], kernels[block, t, 1, r]))
        return carry

    lax.fori_loop(0, ring, one, 0)


def own_kernel(refl, sun, view, azim, flags, _, sums, kernels):
    ring = sums.shape[0]

    def one(i, carry):
        block = sums_part(i, False, ring)
        lanes = lanes_of(block)

        def kernel_of(t, r):
            kvol, kgeo = ross_li(sun[t, r, lanes], view[t, r, lanes], azim[t, r, lanes])
            kernels[block, t, 0, r] = kvol
            kernels[block, t, 1, r] = kgeo
            return kvol, kgeo

        add_dates(sums, i, block, refl, flags, kernel_of)
        return carry

    lax.fori_loop(0, ring, one, 0)


def sums_shapes(refl):
    dates, bands, rows, cols = refl.shape
    parts = cols // LANES
    return [
        jax.ShapeDtypeStruct((parts // 2, 6 + 3 * bands, rows, LANES), jnp.float32),
        jax.ShapeDtypeStruct((parts, dates, 2, rows, LANES), jnp.float32),
    ]


def other_sums(*inputs):
    held = [jax.ShapeDtypeStruct(x.shape, x.dtype) for x in inputs]
    return pl.pallas_call(
        other_kernel,
        in_specs=[pl.BlockSpec(memory_space=pltpu.HBM)] * 5,
        out_specs=[VMEM] * 7,
        out_shape=sums_shapes(inputs[0]) + held,
        scratch_shapes=[pltpu.SemaphoreType.DMA((5, inputs[0].shape[0]))],
        compiler_params=pltpu.CompilerParams(vmem_limit_bytes=16 << 20),
        name="other_sums",
    )(*(pltpu.with_memory_space_constraint(x, pltpu.HBM) for x in inputs))


def own_sums(inputs, kernels):
    return pl.pallas_call(
        own_kernel,
        in_specs=[VMEM] * 6,
        out_specs=[VMEM] * 2,
        out_shape=sums_shapes(inputs[0]),
        input_output_aliases={5: 1},
        compiler_params=pltpu.CompilerParams(vmem_limit_bytes=16 << 20),
        name="own_sums",
    )(*inputs, kernels)


def solve_kernel(own_a, own_b, near, far, smooth, above, below):
    planes, rows, _ = smooth.shape
    bands = planes // 3
    groups = rows // SUB
    for g in range(groups):
        r = slice(g * SUB, (g + 1) * SUB)

        def total(i):
            return (own_a[0, i, r] + own_b[0, i, r]) + (near[i, r] + far[i, r])

        n00 = total(0) + ridge_weight
        n01 = total(1)
        n02 = total(2)
        n11 = total(3) + ridge_weight
        n12 = total(4)
        n22 = total(5) + ridge_weight
        c00 = n11 * n22 - n12 * n12
        c01 = n02 * n12 - n01 * n22
        c02 = n01 * n12 - n02 * n11
        c11 = n00 * n22 - n02 * n02
        c12 = n01 * n02 - n00 * n12
        c22 = n00 * n11 - n01 * n01
        inv_det = 1.0 / (n00 * c00 + n01 * c01 + n02 * c02)
        for b in range(bands):
            x, y, z = total(6 + b), total(6 + bands + b), total(6 + 2 * bands + b)
            smooth[b, r] = (c00 * x + c01 * y + c02 * z) * inv_det
            smooth[bands + b, r] = (c01 * x + c11 * y + c12 * z) * inv_det
            smooth[2 * bands + b, r] = (c02 * x + c12 * y + c22 * z) * inv_det
    row = lax.broadcasted_iota(jnp.int32, (SUB, LANES), 0)
    first, last = row == 0, row == SUB - 1
    zero = jnp.zeros((SUB, LANES), jnp.float32)
    above[...] = jnp.zeros(above.shape, jnp.float32)
    below[...] = jnp.zeros(below.shape, jnp.float32)
    for p in range(planes):
        x = [smooth[p, g * SUB : (g + 1) * SUB] for g in range(groups)]
        below[0, p : p + 1] = x[0][:1] * 0.25
        above[0, p : p + 1] = x[-1][SUB - 1 :] * 0.25
        for g in range(groups):
            prior = jnp.where(last, x[g - 1] if g else zero, x[g])
            later = jnp.where(first, x[g + 1] if g < groups - 1 else zero, x[g])
            y = (pltpu.roll(prior, 1, 0) + 2.0 * x[g] + pltpu.roll(later, SUB - 1, 0)) * 0.25
            smooth[p, g * SUB : (g + 1) * SUB] = y


def solve(own_a, own_b, near, far, bands):
    rows = own_a.shape[2]
    shape = lambda *dims: jax.ShapeDtypeStruct(dims, jnp.float32)
    return pl.pallas_call(
        solve_kernel,
        in_specs=[VMEM] * 4,
        out_specs=[VMEM] * 3,
        out_shape=[shape(3 * bands, rows, LANES)] + [shape(1, rows, LANES)] * 2,
        compiler_params=pltpu.CompilerParams(vmem_limit_bytes=16 << 20),
        name="solve",
    )(own_a, own_b, near, far)


def correct_kernel(refl, kernels, nadir, *rest):
    (halos, pieces), (out, strip) = (rest[:5], rest[5:-2]), rest[-2:]
    step = pl.program_id(0)
    parts = pl.num_programs(0)
    dates, bands, rows, _ = out.shape
    planes, ring = 3 * bands, parts // 2

    @pl.when(step == 0)
    def _():
        strip[0] = jnp.zeros(strip.shape[1:], jnp.float32)
        strip[parts + 1] = jnp.zeros(strip.shape[1:], jnp.float32)
        place, core, way = ring_place()
        own, partner, behind, ahead, beyond = halos
        for (by, flip), piece, (halo, at) in zip(
            (
                (0, 0), (-way, 0), (-way, 1), (-2 * way, 0),
                (0, 1), (way, 1), (way, 0), (2 * way, 1),
            ),
            pieces,
            (
                (own, 0), (behind, 0), (behind, 2), (beyond, 0),
                (partner, 0), (ahead, 0), (ahead, 2), (beyond, 2),
            ),
        ):
            spot = part_at(place + by, 1 - core if flip else core, ring) + 1
            for p in range(planes):
                strip[spot, p] = piece[p]
                strip[spot, p, :1] += halo[at, p : p + 1]
                strip[spot, p, rows - 1 :] += halo[at + 1, p : p + 1]

    lanes = lanes_of(step)
    lane = lax.broadcasted_iota(jnp.int32, (SUB, LANES), 1)
    first, last = lane == 0, lane == LANES - 1
    for g in range(rows // SUB):
        r = slice(g * SUB, (g + 1) * SUB)
        kvol_n, kgeo_n = ross_li_nadir(nadir[r, lanes])

        def smooth(p):
            x = strip[step + 1, p, r]
            prior = pltpu.roll(jnp.where(last, strip[step, p, r], x), 1, 1)
            later = pltpu.roll(jnp.where(first, strip[step + 2, p, r], x), LANES - 1, 1)
            return (prior + 2.0 * x + later) * 0.25

        for b in range(bands):
            iso, vol, geo = smooth(b), smooth(bands + b), smooth(2 * bands + b)
            model_n = iso + vol * kvol_n + geo * kgeo_n
            for t in range(dates):
                model = iso + vol * kernels[step, t, 0, r] + geo * kernels[step, t, 1, r]
                out[t, b, r] = refl[t, b, r, lanes] * model_n / jnp.maximum(model, model_floor)


def correct(refl, kernels, nadir, halos, pieces):
    dates, bands, rows, cols = refl.shape
    parts = cols // LANES
    return pl.pallas_call(
        correct_kernel,
        grid=(parts,),
        in_specs=[VMEM] * (3 + len(halos) + len(pieces)),
        out_specs=pl.BlockSpec((dates, bands, rows, LANES), lambda i: (0, 0, 0, i)),
        scratch_shapes=[pltpu.VMEM((parts + 2, 3 * bands, rows, LANES), jnp.float32)],
        out_shape=jax.ShapeDtypeStruct(refl.shape, jnp.float32),
        compiler_params=pltpu.CompilerParams(vmem_limit_bytes=24 << 20),
        name="correct",
    )(refl, kernels, nadir, *halos, *pieces)


def per_device(reflectance, sun_zenith, view_zenith, rel_azimuth, flags, nadir_sun):
    devices = lax.axis_size("dates")
    bands = reflectance.shape[1]

    def onward(x):
        pairs = [(i, (i + 2 - 4 * (i % 2)) % devices) for i in range(devices)]
        return lax.ppermute(x, "dates", pairs)

    def swap(x):
        return lax.ppermute(x, "dates", [(i, i ^ 1) for i in range(devices)])

    other, kernels, *held = other_sums(reflectance, sun_zenith, view_zenith, rel_azimuth, flags)
    other = swap(other)
    mine, kernels = own_sums(held, kernels)
    far = onward(mine[3] + other[3])
    near = onward(mine[2] + other[2])
    far = onward(mine[1] + other[1] + far)
    near = swap(near)
    own, above, below = solve(mine, other, near, far, bands)

    behind = onward(own)
    partner = swap(own)
    behind_partner = onward(partner)
    relayed = onward(behind)
    pieces = (own, behind, behind_partner, relayed, partner)
    pieces += (swap(behind), swap(behind_partner), swap(relayed))

    blocks = lax.axis_size("rows")
    above = lax.ppermute(above, "rows", [(i, i + 1) for i in range(blocks - 1)])
    below = lax.ppermute(below, "rows", [(i + 1, i) for i in range(blocks - 1)])
    halo = jnp.concatenate([above, below], 0)
    halo_partner = swap(halo)
    halo_both = jnp.concatenate([halo, halo_partner], 0)
    halo_behind = onward(halo_both)
    halo_far = lax.ppermute(
        halo_both, "dates", [(i, (i + devices // 2) % devices) for i in range(devices)]
    )
    halos = (halo, halo_partner, halo_behind, swap(halo_behind), halo_far)
    return correct(held[0], kernels, nadir_sun, halos, pieces)


def solution(mesh):
    in_specs = (
        P("dates", None, "rows", None),
        P("dates", "rows", None),
        P("dates", "rows", None),
        P("dates", "rows", None),
        P("dates", "rows", None),
        P("rows", None),
    )
    out_specs = P("dates", None, "rows", None)

    return jax.shard_map(
        per_device, mesh=mesh, in_specs=in_specs, out_specs=out_specs, check_vma=False
    )
```

```python
import functools
import math

import jax
import jax.numpy as jnp
from jax import lax
from jax.experimental import pallas as pl
from jax.experimental.pallas import tpu as pltpu
from jax.sharding import PartitionSpec as P

ridge_weight = 0.5
model_floor = 0.35
LANES = 128
SUB = 8
VMEM = pl.BlockSpec(memory_space=pltpu.VMEM)


SIN_SUN = (1.0, -0.1666666643, 0.008333314069, -0.0001983586641, 2.693759761e-06)
COS_SUN = (1.0, -0.4999999999, 0.04166666582, -0.001388885292, 2.479463838e-05, -2.693749222e-07)
SIN_VIEW = (1.0, -0.1666664847, 0.008321317392)
COS_VIEW = (1.0, -0.4999987263, 0.04158257081)
SIN_HALF = (1.0, -0.1666666662, 0.008333330977, -0.0001984086155, 2.752528678e-06, -2.388949223e-08)
GEO_POLY = (
    1.570796328, -1.214602072, -0.4109448018, 0.07413550608, -0.02841817795,
    0.01338202682, -0.005993092577, 0.001966222815, -0.0003219403671,
)
VOL_POLY = (
    0.999999995, -1.070795655, 0.08958698627, -0.02642109245, 0.01117480515,
    -0.004945099414, 0.001698688062, -0.0002986314728,
)


def poly(x, coefs):
    total = jnp.full_like(x, coefs[-1])
    for c in coefs[-2::-1]:
        total = total * x + c
    return total


def sin_cos_sun(sun):
    sq = sun * sun
    return sun * poly(sq, SIN_SUN), poly(sq, COS_SUN)


def shadow_term(cos_shadow):
    return jnp.sqrt(1.0 - cos_shadow) * poly(cos_shadow, GEO_POLY)


def ross_li(sun, view, azim):
    sin_s, cos_s = sin_cos_sun(sun)
    view_sq = view * view
    sin_v = view * poly(view_sq, SIN_VIEW)
    cos_v = poly(view_sq, COS_VIEW)
    half = 0.5 * azim
    sin_h = half * poly(half * half, SIN_HALF)
    half_sq = sin_h * sin_h
    cos_a = 1.0 - 2.0 * half_sq
    sin_a_sq = 4.0 * half_sq * (1.0 - half_sq)
    cos_cos = cos_s * cos_v
    sin_sin = sin_s * sin_v
    cos_phase = jnp.clip(cos_cos + sin_sin * cos_a, -1.0, 1.0)
    cos_sum = cos_s + cos_v
    inv = 1.0 / (cos_cos * cos_sum)
    sec_sec = cos_sum * inv
    inv_sum = cos_cos * inv
    kvol = (
        (0.5 * math.pi) * cos_phase + jnp.sqrt(1.0 - cos_phase) * poly(cos_phase, VOL_POLY)
    ) * inv_sum - 0.25 * math.pi
    tan_s = sin_s * cos_v
    tan_v = sin_v * cos_s
    dist_sq = jnp.maximum(tan_s * tan_s + tan_v * tan_v - 2.0 * tan_s * tan_v * cos_a, 0.0)
    cross_sq = sin_sin * sin_sin * sin_a_sq
    cos_shadow = jnp.clip(2.0 * jnp.sqrt(dist_sq + cross_sq) * inv_sum, -1.0, 1.0)
    kgeo = sec_sec * (
        cos_sum * (shadow_term(cos_shadow) * (1.0 / math.pi) - 1.0) + 0.5 * (1.0 + cos_phase)
    )
    return kvol, kgeo


def ross_li_nadir(sun):
    sin_s, cos_s = sin_cos_sun(sun)
    cos_sum = cos_s + 1.0
    inv = 1.0 / (cos_s * cos_sum)
    sec_s = cos_sum * inv
    inv_sum = cos_s * inv
    kvol = ((0.5 * math.pi - sun) * cos_s + sin_s) * inv_sum - 0.25 * math.pi
    cos_shadow = jnp.clip(2.0 * sin_s * inv_sum, -1.0, 1.0)
    kgeo = sec_s * (
        cos_sum * (shadow_term(cos_shadow) * (1.0 / math.pi) - 1.0) + 0.5 * (1.0 + cos_s)
    )
    return kvol, kgeo


def ring_place():
    index = lax.axis_index("dates")
    core = lax.rem(index, 2)
    return lax.div(index, 2), core, 1 - 2 * core


def part_at(place, core, ring):
    return core * ring + lax.rem(place + 2 * ring, ring)


def sums_part(i, flip, ring):
    place, core, way = ring_place()
    if flip:
        core, way = 1 - core, -way
    by = jnp.where(i == 0, 0, jnp.where(i == 3, 2, way))
    return part_at(place + by, jnp.where(i == 2, 1 - core, core), ring)


def lanes_of(part):
    return pl.ds(pl.multiple_of(part * LANES, LANES), LANES)


def weight_of(f):
    weight = jnp.where(f == 1, 0.3, jnp.where(f == 2, 0.7, jnp.where(f == 3, 1.0, 0.0)))
    return weight.astype(jnp.float32)


def add_dates(sums, part, block, refl, flags, kernel_of):
    dates, bands, rows, _ = refl.shape
    lanes = lanes_of(block)
    for g in range(rows // SUB):
        r = slice(g * SUB, (g + 1) * SUB)
        acc = [None] * (6 + 3 * bands)

        def add(i, x):
            acc[i] = x if acc[i] is None else acc[i] + x

        for t in range(dates):
            kvol, kgeo = kernel_of(t, r)
            weight = weight_of(flags[t, r, lanes])
            wvol = weight * kvol
            wgeo = weight * kgeo
            for i, x in enumerate((weight, wvol, wgeo, wvol * kvol, wvol * kgeo, wgeo * kgeo)):
                add(i, x)
            for b in range(bands):
                x = refl[t, b, r, lanes]
                add(6 + b, weight * x)
                add(6 + bands + b, wvol * x)
                add(6 + 2 * bands + b, wgeo * x)
        for i, x in enumerate(acc):
            sums[part, i, r] = x


def copies_in(sources, held, sems):
    dates = held[0].shape[0]
    for k in (1, 2, 3, 4, 0):
        for t in range(dates):
            pltpu.make_async_copy(sources[k].at[t], held[k].at[t], sems.at[k, t]).start()

    def wait(k, t):
        pltpu.make_async_copy(sources[k].at[t], held[k].at[t], sems.at[k, t]).wait()

    return wait


def far_kernel(*refs):
    sources, sums, kernels, held, sems = refs[:5], refs[5:7], refs[7], refs[8:13], refs[13]
    refl, sun, view, azim, flags = held
    dates, _, rows, cols = refl.shape
    ring = cols // LANES // 2
    wait = copies_in(sources, held, sems)
    blocks = [sums_part(3, flip, ring) for flip in (True, False)]
    for t in range(dates):
        for k in (1, 2, 3):
            wait(k, t)
        for block in blocks:
            lanes = lanes_of(block)
            for g in range(rows // SUB):
                r = slice(g * SUB, (g + 1) * SUB)
                kvol, kgeo = ross_li(sun[t, r, lanes], view[t, r, lanes], azim[t, r, lanes])
                kernels[block, t, 0, r] = kvol
                kernels[block, t, 1, r] = kgeo
    for k in (4, 0):
        for t in range(dates):
            wait(k, t)
    for block, total in zip(blocks, sums):
        kernel_of = lambda t, r: (kernels[block, t, 0, r], kernels[block, t, 1, r])
        add_dates(total, 0, block, refl, flags, kernel_of)


def rest_kernel(flip, refl, sun, view, azim, flags, _, sums, kernels):
    ring = refl.shape[3] // LANES // 2

    def one(i, carry):
        block = sums_part(i, flip, ring)
        lanes = lanes_of(block)

        def kernel_of(t, r):
            kvol, kgeo = ross_li(sun[t, r, lanes], view[t, r, lanes], azim[t, r, lanes])
            kernels[block, t, 0, r] = kvol
            kernels[block, t, 1, r] = kgeo
            return kvol, kgeo

        add_dates(sums, i, block, refl, flags, kernel_of)
        return carry

    lax.fori_loop(0, ring - 1, one, 0)


def sums_shape(refl, parts):
    _, bands, rows, _ = refl.shape
    return jax.ShapeDtypeStruct((parts, 6 + 3 * bands, rows, LANES), jnp.float32)


def kernels_shape(refl):
    dates, _, rows, cols = refl.shape
    return jax.ShapeDtypeStruct((cols // LANES, dates, 2, rows, LANES), jnp.float32)


def far_sums(*inputs):
    refl = inputs[0]
    held = [jax.ShapeDtypeStruct(x.shape, x.dtype) for x in inputs]
    return pl.pallas_call(
        far_kernel,
        in_specs=[pl.BlockSpec(memory_space=pltpu.HBM)] * 5,
        out_specs=[VMEM] * 8,
        out_shape=[sums_shape(refl, 1), sums_shape(refl, 1), kernels_shape(refl)] + held,
        scratch_shapes=[pltpu.SemaphoreType.DMA((5, refl.shape[0]))],
        compiler_params=pltpu.CompilerParams(vmem_limit_bytes=16 << 20),
        name="far_sums",
    )(*(pltpu.with_memory_space_constraint(x, pltpu.HBM) for x in inputs))


def rest_sums(flip, inputs, kernels):
    refl = inputs[0]
    ring = refl.shape[3] // LANES // 2
    return pl.pallas_call(
        functools.partial(rest_kernel, flip),
        in_specs=[VMEM] * 6,
        out_specs=[VMEM] * 2,
        out_shape=[sums_shape(refl, ring - 1), kernels_shape(refl)],
        input_output_aliases={5: 1},
        compiler_params=pltpu.CompilerParams(vmem_limit_bytes=16 << 20),
    )(*inputs, kernels)


def solve_kernel(own_a, own_b, near, far, smooth, above, below):
    planes, rows, _ = smooth.shape
    bands = planes // 3
    groups = rows // SUB
    for g in range(groups):
        r = slice(g * SUB, (g + 1) * SUB)

        def total(i):
            return (own_a[0, i, r] + own_b[0, i, r]) + (near[i, r] + far[i, r])

        n00 = total(0) + ridge_weight
        n01 = total(1)
        n02 = total(2)
        n11 = total(3) + ridge_weight
        n12 = total(4)
        n22 = total(5) + ridge_weight
        c00 = n11 * n22 - n12 * n12
        c01 = n02 * n12 - n01 * n22
        c02 = n01 * n12 - n02 * n11
        c11 = n00 * n22 - n02 * n02
        c12 = n01 * n02 - n00 * n12
        c22 = n00 * n11 - n01 * n01
        inv_det = 1.0 / (n00 * c00 + n01 * c01 + n02 * c02)
        for b in range(bands):
            x, y, z = total(6 + b), total(6 + bands + b), total(6 + 2 * bands + b)
            smooth[b, r] = (c00 * x + c01 * y + c02 * z) * inv_det
            smooth[bands + b, r] = (c01 * x + c11 * y + c12 * z) * inv_det
            smooth[2 * bands + b, r] = (c02 * x + c12 * y + c22 * z) * inv_det
    row = lax.broadcasted_iota(jnp.int32, (SUB, LANES), 0)
    first, last = row == 0, row == SUB - 1
    zero = jnp.zeros((SUB, LANES), jnp.float32)
    above[...] = jnp.zeros(above.shape, jnp.float32)
    below[...] = jnp.zeros(below.shape, jnp.float32)
    for p in range(planes):
        x = [smooth[p, g * SUB : (g + 1) * SUB] for g in range(groups)]
        below[0, p : p + 1] = x[0][:1] * 0.25
        above[0, p : p + 1] = x[-1][SUB - 1 :] * 0.25
        for g in range(groups):
            prior = jnp.where(last, x[g - 1] if g else zero, x[g])
            later = jnp.where(first, x[g + 1] if g < groups - 1 else zero, x[g])
            y = (pltpu.roll(prior, 1, 0) + 2.0 * x[g] + pltpu.roll(later, SUB - 1, 0)) * 0.25
            smooth[p, g * SUB : (g + 1) * SUB] = y


def solve(own_a, own_b, near, far, bands):
    rows = own_a.shape[2]
    shape = lambda *dims: jax.ShapeDtypeStruct(dims, jnp.float32)
    return pl.pallas_call(
        solve_kernel,
        in_specs=[VMEM] * 4,
        out_specs=[VMEM] * 3,
        out_shape=[shape(3 * bands, rows, LANES)] + [shape(1, rows, LANES)] * 2,
        compiler_params=pltpu.CompilerParams(vmem_limit_bytes=16 << 20),
        name="solve",
    )(own_a, own_b, near, far)


def correct_kernel(refl, kernels, nadir, *rest):
    (halos, pieces), (out, strip) = (rest[:5], rest[5:-2]), rest[-2:]
    step = pl.program_id(0)
    parts = pl.num_programs(0)
    dates, bands, rows, _ = out.shape
    planes, ring = 3 * bands, parts // 2

    @pl.when(step == 0)
    def _():
        strip[0] = jnp.zeros(strip.shape[1:], jnp.float32)
        strip[parts + 1] = jnp.zeros(strip.shape[1:], jnp.float32)
        place, core, way = ring_place()
        own, partner, behind, ahead, beyond = halos
        for (by, flip), piece, (halo, at) in zip(
            (
                (0, 0), (-way, 0), (-way, 1), (-2 * way, 0),
                (0, 1), (way, 1), (way, 0), (2 * way, 1),
            ),
            pieces,
            (
                (own, 0), (behind, 0), (behind, 2), (beyond, 0),
                (partner, 0), (ahead, 0), (ahead, 2), (beyond, 2),
            ),
        ):
            spot = part_at(place + by, 1 - core if flip else core, ring) + 1
            for p in range(planes):
                strip[spot, p] = piece[p]
                strip[spot, p, :1] += halo[at, p : p + 1]
                strip[spot, p, rows - 1 :] += halo[at + 1, p : p + 1]

    lanes = lanes_of(step)
    lane = lax.broadcasted_iota(jnp.int32, (SUB, LANES), 1)
    first, last = lane == 0, lane == LANES - 1
    for g in range(rows // SUB):
        r = slice(g * SUB, (g + 1) * SUB)
        kvol_n, kgeo_n = ross_li_nadir(nadir[r, lanes])

        def smooth(p):
            x = strip[step + 1, p, r]
            prior = pltpu.roll(jnp.where(last, strip[step, p, r], x), 1, 1)
            later = pltpu.roll(jnp.where(first, strip[step + 2, p, r], x), LANES - 1, 1)
            return (prior + 2.0 * x + later) * 0.25

        for b in range(bands):
            iso, vol, geo = smooth(b), smooth(bands + b), smooth(2 * bands + b)
            model_n = iso + vol * kvol_n + geo * kgeo_n
            for t in range(dates):
                model = iso + vol * kernels[step, t, 0, r] + geo * kernels[step, t, 1, r]
                out[t, b, r] = refl[t, b, r, lanes] * model_n / jnp.maximum(model, model_floor)


def correct(refl, kernels, nadir, halos, pieces):
    dates, bands, rows, cols = refl.shape
    parts = cols // LANES
    return pl.pallas_call(
        correct_kernel,
        grid=(parts,),
        in_specs=[VMEM] * (3 + len(halos) + len(pieces)),
        out_specs=pl.BlockSpec((dates, bands, rows, LANES), lambda i: (0, 0, 0, i)),
        scratch_shapes=[pltpu.VMEM((parts + 2, 3 * bands, rows, LANES), jnp.float32)],
        out_shape=jax.ShapeDtypeStruct(refl.shape, jnp.float32),
        compiler_params=pltpu.CompilerParams(vmem_limit_bytes=24 << 20),
        name="correct",
    )(refl, kernels, nadir, *halos, *pieces)


def per_device(reflectance, sun_zenith, view_zenith, rel_azimuth, flags, nadir_sun):
    devices = lax.axis_size("dates")
    bands = reflectance.shape[1]

    def onward(x):
        pairs = [(i, (i + 2 - 4 * (i % 2)) % devices) for i in range(devices)]
        return lax.ppermute(x, "dates", pairs)

    def swap(x):
        return lax.ppermute(x, "dates", [(i, i ^ 1) for i in range(devices)])

    inputs = (reflectance, sun_zenith, view_zenith, rel_azimuth, flags)
    far_other, far_mine, kernels, *held = far_sums(*inputs)
    far_other = swap(far_other)
    other, kernels = rest_sums(True, held, kernels)
    other = swap(other)
    far = onward((far_mine + far_other)[0])
    mine, kernels = rest_sums(False, held, kernels)
    near = onward(mine[2] + other[2])
    far = onward(mine[1] + other[1] + far)
    near = swap(near)
    own, above, below = solve(mine, other, near, far, bands)

    behind = onward(own)
    partner = swap(own)
    behind_partner = onward(partner)
    relayed = onward(behind)
    pieces = (own, behind, behind_partner, relayed, partner)
    pieces += (swap(behind), swap(behind_partner), swap(relayed))

    blocks = lax.axis_size("rows")
    above = lax.ppermute(above, "rows", [(i, i + 1) for i in range(blocks - 1)])
    below = lax.ppermute(below, "rows", [(i + 1, i) for i in range(blocks - 1)])
    halo = jnp.concatenate([above, below], 0)
    halo_partner = swap(halo)
    halo_both = jnp.concatenate([halo, halo_partner], 0)
    halo_behind = onward(halo_both)
    halo_far = lax.ppermute(
        halo_both, "dates", [(i, (i + devices // 2) % devices) for i in range(devices)]
    )
    halos = (halo, halo_partner, halo_behind, swap(halo_behind), halo_far)
    return correct(held[0], kernels, nadir_sun, halos, pieces)


def solution(mesh):
    in_specs = (
        P("dates", None, "rows", None),
        P("dates", "rows", None),
        P("dates", "rows", None),
        P("dates", "rows", None),
        P("dates", "rows", None),
        P("rows", None),
    )
    out_specs = P("dates", None, "rows", None)

    return jax.shard_map(
        per_device, mesh=mesh, in_specs=in_specs, out_specs=out_specs, check_vma=False
    )
```

```python
import functools
import math

import jax
import jax.numpy as jnp
from jax import lax
from jax.experimental import pallas as pl
from jax.experimental.pallas import tpu as pltpu
from jax.sharding import PartitionSpec as P

ridge_weight = 0.5
model_floor = 0.35
LANES = 128
SUB = 8
VMEM = pl.BlockSpec(memory_space=pltpu.VMEM)


SIN_SUN = (1.0, -0.1666666643, 0.008333314069, -0.0001983586641, 2.693759761e-06)
COS_SUN = (1.0, -0.4999999999, 0.04166666582, -0.001388885292, 2.479463838e-05, -2.693749222e-07)
SIN_VIEW = (1.0, -0.1666664847, 0.008321317392)
COS_VIEW = (1.0, -0.4999987263, 0.04158257081)
SIN_HALF = (1.0, -0.1666666662, 0.008333330977, -0.0001984086155, 2.752528678e-06, -2.388949223e-08)
GEO_POLY = (
    1.570796328, -1.214602072, -0.4109448018, 0.07413550608, -0.02841817795,
    0.01338202682, -0.005993092577, 0.001966222815, -0.0003219403671,
)
VOL_POLY = (
    0.999999995, -1.070795655, 0.08958698627, -0.02642109245, 0.01117480515,
    -0.004945099414, 0.001698688062, -0.0002986314728,
)


def poly(x, coefs):
    total = jnp.full_like(x, coefs[-1])
    for c in coefs[-2::-1]:
        total = total * x + c
    return total


def sin_cos_sun(sun):
    sq = sun * sun
    return sun * poly(sq, SIN_SUN), poly(sq, COS_SUN)


def shadow_term(cos_shadow):
    return jnp.sqrt(1.0 - cos_shadow) * poly(cos_shadow, GEO_POLY)


def ross_li(sun, view, azim):
    sin_s, cos_s = sin_cos_sun(sun)
    view_sq = view * view
    sin_v = view * poly(view_sq, SIN_VIEW)
    cos_v = poly(view_sq, COS_VIEW)
    half = 0.5 * azim
    sin_h = half * poly(half * half, SIN_HALF)
    half_sq = sin_h * sin_h
    cos_a = 1.0 - 2.0 * half_sq
    sin_a_sq = 4.0 * half_sq * (1.0 - half_sq)
    cos_cos = cos_s * cos_v
    sin_sin = sin_s * sin_v
    cos_phase = jnp.clip(cos_cos + sin_sin * cos_a, -1.0, 1.0)
    cos_sum = cos_s + cos_v
    inv = 1.0 / (cos_cos * cos_sum)
    sec_sec = cos_sum * inv
    inv_sum = cos_cos * inv
    kvol = (
        (0.5 * math.pi) * cos_phase + jnp.sqrt(1.0 - cos_phase) * poly(cos_phase, VOL_POLY)
    ) * inv_sum - 0.25 * math.pi
    tan_s = sin_s * cos_v
    tan_v = sin_v * cos_s
    dist_sq = jnp.maximum(tan_s * tan_s + tan_v * tan_v - 2.0 * tan_s * tan_v * cos_a, 0.0)
    cross_sq = sin_sin * sin_sin * sin_a_sq
    cos_shadow = jnp.clip(2.0 * jnp.sqrt(dist_sq + cross_sq) * inv_sum, -1.0, 1.0)
    kgeo = sec_sec * (
        cos_sum * (shadow_term(cos_shadow) * (1.0 / math.pi) - 1.0) + 0.5 * (1.0 + cos_phase)
    )
    return kvol, kgeo


def ross_li_nadir(sun):
    sin_s, cos_s = sin_cos_sun(sun)
    cos_sum = cos_s + 1.0
    inv = 1.0 / (cos_s * cos_sum)
    sec_s = cos_sum * inv
    inv_sum = cos_s * inv
    kvol = ((0.5 * math.pi - sun) * cos_s + sin_s) * inv_sum - 0.25 * math.pi
    cos_shadow = jnp.clip(2.0 * sin_s * inv_sum, -1.0, 1.0)
    kgeo = sec_s * (
        cos_sum * (shadow_term(cos_shadow) * (1.0 / math.pi) - 1.0) + 0.5 * (1.0 + cos_s)
    )
    return kvol, kgeo


def ring_place():
    index = lax.axis_index("dates")
    core = lax.rem(index, 2)
    return lax.div(index, 2), core, 1 - 2 * core


def part_at(place, core, ring):
    return core * ring + lax.rem(place + 2 * ring, ring)


def sums_part(i, flip, ring):
    place, core, way = ring_place()
    if flip:
        core, way = 1 - core, -way
    by = jnp.where(i == 0, 0, jnp.where(i == 3, 2, way))
    return part_at(place + by, jnp.where(i == 2, 1 - core, core), ring)


def lanes_of(part):
    return pl.ds(pl.multiple_of(part * LANES, LANES), LANES)


def weight_of(f):
    weight = jnp.where(f == 1, 0.3, jnp.where(f == 2, 0.7, jnp.where(f == 3, 1.0, 0.0)))
    return weight.astype(jnp.float32)


def add_dates(sums, part, block, refl, flags, kernel_of):
    dates, bands, rows, _ = refl.shape
    lanes = lanes_of(block)
    for g in range(rows // SUB):
        r = slice(g * SUB, (g + 1) * SUB)
        acc = [None] * (6 + 3 * bands)

        def add(i, x):
            acc[i] = x if acc[i] is None else acc[i] + x

        for t in range(dates):
            kvol, kgeo = kernel_of(t, r)
            weight = weight_of(flags[t, r, lanes])
            wvol = weight * kvol
            wgeo = weight * kgeo
            for i, x in enumerate((weight, wvol, wgeo, wvol * kvol, wvol * kgeo, wgeo * kgeo)):
                add(i, x)
            for b in range(bands):
                x = refl[t, b, r, lanes]
                add(6 + b, weight * x)
                add(6 + bands + b, wvol * x)
                add(6 + 2 * bands + b, wgeo * x)
        for i, x in enumerate(acc):
            sums[part, i, r] = x


def copies_in(sources, held, sems):
    dates = held[0].shape[0]
    for k in (1, 2, 3, 4, 0):
        for t in range(dates):
            pltpu.make_async_copy(sources[k].at[t], held[k].at[t], sems.at[k, t]).start()

    def wait(k, t):
        pltpu.make_async_copy(sources[k].at[t], held[k].at[t], sems.at[k, t]).wait()

    return wait


def far_kernel(*refs):
    sources, sums, kernels, held, sems = refs[:5], refs[5:7], refs[7], refs[8:13], refs[13]
    refl, sun, view, azim, flags = held
    dates, _, rows, cols = refl.shape
    ring = cols // LANES // 2
    wait = copies_in(sources, held, sems)
    blocks = [sums_part(3, flip, ring) for flip in (True, False)]
    for t in range(dates):
        for k in (1, 2, 3):
            wait(k, t)
        for block in blocks:
            lanes = lanes_of(block)
            for g in range(rows // SUB):
                r = slice(g * SUB, (g + 1) * SUB)
                kvol, kgeo = ross_li(sun[t, r, lanes], view[t, r, lanes], azim[t, r, lanes])
                kernels[block, t, 0, r] = kvol
                kernels[block, t, 1, r] = kgeo
    for k in (4, 0):
        for t in range(dates):
            wait(k, t)
    for block, total in zip(blocks, sums):
        kernel_of = lambda t, r: (kernels[block, t, 0, r], kernels[block, t, 1, r])
        add_dates(total, 0, block, refl, flags, kernel_of)


def rest_kernel(flip, refl, sun, view, azim, flags, _, sums, kernels):
    ring = refl.shape[3] // LANES // 2

    def one(i, carry):
        block = sums_part(i, flip, ring)
        lanes = lanes_of(block)

        def kernel_of(t, r):
            kvol, kgeo = ross_li(sun[t, r, lanes], view[t, r, lanes], azim[t, r, lanes])
            kernels[block, t, 0, r] = kvol
            kernels[block, t, 1, r] = kgeo
            return kvol, kgeo

        add_dates(sums, i, block, refl, flags, kernel_of)
        return carry

    lax.fori_loop(0, ring - 1, one, 0)


def sums_shape(refl, parts):
    _, bands, rows, _ = refl.shape
    return jax.ShapeDtypeStruct((parts, 6 + 3 * bands, rows, LANES), jnp.float32)


def kernels_shape(refl):
    dates, _, rows, cols = refl.shape
    return jax.ShapeDtypeStruct((cols // LANES, dates, 2, rows, LANES), jnp.float32)


def far_sums(*inputs):
    refl = inputs[0]
    held = [jax.ShapeDtypeStruct(x.shape, x.dtype) for x in inputs]
    return pl.pallas_call(
        far_kernel,
        in_specs=[pl.BlockSpec(memory_space=pltpu.HBM)] * 5,
        out_specs=[VMEM] * 8,
        out_shape=[sums_shape(refl, 1), sums_shape(refl, 1), kernels_shape(refl)] + held,
        scratch_shapes=[pltpu.SemaphoreType.DMA((5, refl.shape[0]))],
        compiler_params=pltpu.CompilerParams(vmem_limit_bytes=16 << 20),
        name="far_sums",
    )(*(pltpu.with_memory_space_constraint(x, pltpu.HBM) for x in inputs))


def rest_sums(flip, inputs, kernels):
    refl = inputs[0]
    ring = refl.shape[3] // LANES // 2
    return pl.pallas_call(
        functools.partial(rest_kernel, flip),
        in_specs=[VMEM] * 6,
        out_specs=[VMEM] * 2,
        out_shape=[sums_shape(refl, ring - 1), kernels_shape(refl)],
        input_output_aliases={5: 1},
        compiler_params=pltpu.CompilerParams(vmem_limit_bytes=16 << 20),
    )(*inputs, kernels)


def solve_kernel(own_a, own_b, near, far, smooth, above, below):
    planes, rows, _ = smooth.shape
    bands = planes // 3
    groups = rows // SUB
    for g in range(groups):
        r = slice(g * SUB, (g + 1) * SUB)

        def total(i):
            return (own_a[0, i, r] + own_b[0, i, r]) + (near[i, r] + far[i, r])

        n00 = total(0) + ridge_weight
        n01 = total(1)
        n02 = total(2)
        n11 = total(3) + ridge_weight
        n12 = total(4)
        n22 = total(5) + ridge_weight
        c00 = n11 * n22 - n12 * n12
        c01 = n02 * n12 - n01 * n22
        c02 = n01 * n12 - n02 * n11
        c11 = n00 * n22 - n02 * n02
        c12 = n01 * n02 - n00 * n12
        c22 = n00 * n11 - n01 * n01
        inv_det = 1.0 / (n00 * c00 + n01 * c01 + n02 * c02)
        for b in range(bands):
            x, y, z = total(6 + b), total(6 + bands + b), total(6 + 2 * bands + b)
            smooth[b, r] = (c00 * x + c01 * y + c02 * z) * inv_det
            smooth[bands + b, r] = (c01 * x + c11 * y + c12 * z) * inv_det
            smooth[2 * bands + b, r] = (c02 * x + c12 * y + c22 * z) * inv_det
    row = lax.broadcasted_iota(jnp.int32, (SUB, LANES), 0)
    first, last = row == 0, row == SUB - 1
    zero = jnp.zeros((SUB, LANES), jnp.float32)
    above[...] = jnp.zeros(above.shape, jnp.float32)
    below[...] = jnp.zeros(below.shape, jnp.float32)
    for p in range(planes):
        x = [smooth[p, g * SUB : (g + 1) * SUB] for g in range(groups)]
        below[0, p : p + 1] = x[0][:1] * 0.0625
        above[0, p : p + 1] = x[-1][SUB - 1 :] * 0.0625
        for g in range(groups):
            prior = jnp.where(last, x[g - 1] if g else zero, x[g])
            later = jnp.where(first, x[g + 1] if g < groups - 1 else zero, x[g])
            y = (pltpu.roll(prior, 1, 0) + 2.0 * x[g] + pltpu.roll(later, SUB - 1, 0)) * 0.0625
            smooth[p, g * SUB : (g + 1) * SUB] = y


def solve(own_a, own_b, near, far, bands):
    rows = own_a.shape[2]
    shape = lambda *dims: jax.ShapeDtypeStruct(dims, jnp.float32)
    return pl.pallas_call(
        solve_kernel,
        in_specs=[VMEM] * 4,
        out_specs=[VMEM] * 3,
        out_shape=[shape(3 * bands, rows, LANES)] + [shape(1, rows, LANES)] * 2,
        compiler_params=pltpu.CompilerParams(vmem_limit_bytes=16 << 20),
        name="solve",
    )(own_a, own_b, near, far)


def correct_kernel(refl, kernels, nadir, *rest):
    (halos, pieces), (out, strip) = (rest[:5], rest[5:-2]), rest[-2:]
    step = pl.program_id(0)
    parts = pl.num_programs(0)
    dates, bands, rows, _ = out.shape
    planes, ring = 3 * bands, parts // 2

    @pl.when(step == 0)
    def _():
        strip[0] = jnp.zeros(strip.shape[1:], jnp.float32)
        strip[parts + 1] = jnp.zeros(strip.shape[1:], jnp.float32)
        place, core, way = ring_place()
        own, partner, behind, ahead, beyond = halos
        for (by, flip), piece, (halo, at) in zip(
            (
                (0, 0), (-way, 0), (-way, 1), (-2 * way, 0),
                (0, 1), (way, 1), (way, 0), (2 * way, 1),
            ),
            pieces,
            (
                (own, 0), (behind, 0), (behind, 2), (beyond, 0),
                (partner, 0), (ahead, 0), (ahead, 2), (beyond, 2),
            ),
        ):
            spot = part_at(place + by, 1 - core if flip else core, ring) + 1
            for p in range(planes):
                strip[spot, p] = piece[p]
                strip[spot, p, :1] += halo[at, p : p + 1]
                strip[spot, p, rows - 1 :] += halo[at + 1, p : p + 1]

    lanes = lanes_of(step)
    lane = lax.broadcasted_iota(jnp.int32, (SUB, LANES), 1)
    first, last = lane == 0, lane == LANES - 1
    for g in range(rows // SUB):
        r = slice(g * SUB, (g + 1) * SUB)
        kvol_n, kgeo_n = ross_li_nadir(nadir[r, lanes])

        def smooth(p):
            x = strip[step + 1, p, r]
            prior = pltpu.roll(jnp.where(last, strip[step, p, r], x), 1, 1)
            later = pltpu.roll(jnp.where(first, strip[step + 2, p, r], x), LANES - 1, 1)
            return prior + 2.0 * x + later

        for b in range(bands):
            iso, vol, geo = smooth(b), smooth(bands + b), smooth(2 * bands + b)
            model_n = iso + vol * kvol_n + geo * kgeo_n
            for t in range(dates):
                model = iso + vol * kernels[step, t, 0, r] + geo * kernels[step, t, 1, r]
                out[t, b, r] = refl[t, b, r, lanes] * model_n / jnp.maximum(model, model_floor)


def correct(refl, kernels, nadir, halos, pieces):
    dates, bands, rows, cols = refl.shape
    parts = cols // LANES
    return pl.pallas_call(
        correct_kernel,
        grid=(parts,),
        in_specs=[VMEM] * (3 + len(halos) + len(pieces)),
        out_specs=pl.BlockSpec((dates, bands, rows, LANES), lambda i: (0, 0, 0, i)),
        scratch_shapes=[pltpu.VMEM((parts + 2, 3 * bands, rows, LANES), jnp.float32)],
        out_shape=jax.ShapeDtypeStruct(refl.shape, jnp.float32),
        compiler_params=pltpu.CompilerParams(vmem_limit_bytes=24 << 20),
        name="correct",
    )(refl, kernels, nadir, *halos, *pieces)


def per_device(reflectance, sun_zenith, view_zenith, rel_azimuth, flags, nadir_sun):
    devices = lax.axis_size("dates")
    bands = reflectance.shape[1]

    def onward(x):
        pairs = [(i, (i + 2 - 4 * (i % 2)) % devices) for i in range(devices)]
        return lax.ppermute(x, "dates", pairs)

    def swap(x):
        return lax.ppermute(x, "dates", [(i, i ^ 1) for i in range(devices)])

    inputs = (reflectance, sun_zenith, view_zenith, rel_azimuth, flags)
    far_other, far_mine, kernels, *held = far_sums(*inputs)
    far_other = swap(far_other)
    other, kernels = rest_sums(True, held, kernels)
    other = swap(other)
    far = onward((far_mine + far_other)[0])
    mine, kernels = rest_sums(False, held, kernels)
    near = onward(mine[2] + other[2])
    far = onward(mine[1] + other[1] + far)
    near = swap(near)
    own, above, below = solve(mine, other, near, far, bands)

    behind = onward(own)
    partner = swap(own)
    behind_partner = onward(partner)
    relayed = onward(behind)
    pieces = (own, behind, behind_partner, relayed, partner)
    pieces += (swap(behind), swap(behind_partner), swap(relayed))

    blocks = lax.axis_size("rows")
    above = lax.ppermute(above, "rows", [(i, i + 1) for i in range(blocks - 1)])
    below = lax.ppermute(below, "rows", [(i + 1, i) for i in range(blocks - 1)])
    halo = jnp.concatenate([above, below], 0)
    halo_partner = swap(halo)
    halo_both = jnp.concatenate([halo, halo_partner], 0)
    halo_behind = onward(halo_both)
    halo_far = lax.ppermute(
        halo_both, "dates", [(i, (i + devices // 2) % devices) for i in range(devices)]
    )
    halos = (halo, halo_partner, halo_behind, swap(halo_behind), halo_far)
    return correct(held[0], kernels, nadir_sun, halos, pieces)


def solution(mesh):
    in_specs = (
        P("dates", None, "rows", None),
        P("dates", "rows", None),
        P("dates", "rows", None),
        P("dates", "rows", None),
        P("dates", "rows", None),
        P("rows", None),
    )
    out_specs = P("dates", None, "rows", None)

    return jax.shard_map(
        per_device, mesh=mesh, in_specs=in_specs, out_specs=out_specs, check_vma=False
    )
```

```python
import functools
import math

import jax
import jax.numpy as jnp
from jax import lax
from jax.experimental import pallas as pl
from jax.experimental.pallas import tpu as pltpu
from jax.sharding import PartitionSpec as P

ridge_weight = 0.5
model_floor = 0.35
LANES = 128
SUB = 8
VMEM = pl.BlockSpec(memory_space=pltpu.VMEM)


SIN_SUN = (1.0, -0.1666666643, 0.008333314069, -0.0001983586641, 2.693759761e-06)
COS_SUN = (1.0, -0.4999999999, 0.04166666582, -0.001388885292, 2.479463838e-05, -2.693749222e-07)
SIN_VIEW = (1.0, -0.1666664847, 0.008321317392)
COS_VIEW = (1.0, -0.4999987263, 0.04158257081)
SIN_HALF = (1.0, -0.1666666662, 0.008333330977, -0.0001984086155, 2.752528678e-06, -2.388949223e-08)
GEO_POLY = (
    1.570796328, -1.214602072, -0.4109448018, 0.07413550608, -0.02841817795,
    0.01338202682, -0.005993092577, 0.001966222815, -0.0003219403671,
)
VOL_POLY = (
    0.999999995, -1.070795655, 0.08958698627, -0.02642109245, 0.01117480515,
    -0.004945099414, 0.001698688062, -0.0002986314728,
)


def poly(x, coefs):
    total = jnp.full_like(x, coefs[-1])
    for c in coefs[-2::-1]:
        total = total * x + c
    return total


def sin_cos_sun(sun):
    sq = sun * sun
    return sun * poly(sq, SIN_SUN), poly(sq, COS_SUN)


def shadow_term(cos_shadow):
    return jnp.sqrt(1.0 - cos_shadow) * poly(cos_shadow, GEO_POLY)


def ross_li(sun, view, azim):
    sin_s, cos_s = sin_cos_sun(sun)
    view_sq = view * view
    sin_v = view * poly(view_sq, SIN_VIEW)
    cos_v = poly(view_sq, COS_VIEW)
    half = 0.5 * azim
    sin_h = half * poly(half * half, SIN_HALF)
    half_sq = sin_h * sin_h
    cos_a = 1.0 - 2.0 * half_sq
    sin_a_sq = 4.0 * half_sq * (1.0 - half_sq)
    cos_cos = cos_s * cos_v
    sin_sin = sin_s * sin_v
    cos_phase = jnp.clip(cos_cos + sin_sin * cos_a, -1.0, 1.0)
    cos_sum = cos_s + cos_v
    inv = 1.0 / (cos_cos * cos_sum)
    sec_sec = cos_sum * inv
    inv_sum = cos_cos * inv
    kvol = (
        (0.5 * math.pi) * cos_phase + jnp.sqrt(1.0 - cos_phase) * poly(cos_phase, VOL_POLY)
    ) * inv_sum - 0.25 * math.pi
    tan_s = sin_s * cos_v
    tan_v = sin_v * cos_s
    dist_sq = jnp.maximum(tan_s * tan_s + tan_v * tan_v - 2.0 * tan_s * tan_v * cos_a, 0.0)
    cross_sq = sin_sin * sin_sin * sin_a_sq
    cos_shadow = jnp.clip(2.0 * jnp.sqrt(dist_sq + cross_sq) * inv_sum, -1.0, 1.0)
    kgeo = sec_sec * (
        cos_sum * (shadow_term(cos_shadow) * (1.0 / math.pi) - 1.0) + 0.5 * (1.0 + cos_phase)
    )
    return kvol, kgeo


def ross_li_nadir(sun):
    sin_s, cos_s = sin_cos_sun(sun)
    cos_sum = cos_s + 1.0
    inv = 1.0 / (cos_s * cos_sum)
    sec_s = cos_sum * inv
    inv_sum = cos_s * inv
    kvol = ((0.5 * math.pi - sun) * cos_s + sin_s) * inv_sum - 0.25 * math.pi
    cos_shadow = jnp.clip(2.0 * sin_s * inv_sum, -1.0, 1.0)
    kgeo = sec_s * (
        cos_sum * (shadow_term(cos_shadow) * (1.0 / math.pi) - 1.0) + 0.5 * (1.0 + cos_s)
    )
    return kvol, kgeo


def ring_place():
    index = lax.axis_index("dates")
    core = lax.rem(index, 2)
    return lax.div(index, 2), core, 1 - 2 * core


def part_at(place, core, ring):
    return core * ring + lax.rem(place + 2 * ring, ring)


def sums_part(i, flip, ring):
    place, core, way = ring_place()
    if flip:
        core, way = 1 - core, -way
    by = jnp.where(i == 0, 0, jnp.where(i == 3, 2, way))
    return part_at(place + by, jnp.where(i == 2, 1 - core, core), ring)


def lanes_of(part):
    return pl.ds(pl.multiple_of(part * LANES, LANES), LANES)


def weight_of(f):
    weight = jnp.where(f == 1, 0.3, jnp.where(f == 2, 0.7, jnp.where(f == 3, 1.0, 0.0)))
    return weight.astype(jnp.float32)


def add_dates(sums, part, block, refl, flags, kernel_of):
    dates, bands, rows, _ = refl.shape
    lanes = lanes_of(block)
    for g in range(rows // SUB):
        r = slice(g * SUB, (g + 1) * SUB)
        acc = [None] * (6 + 3 * bands)

        def add(i, x):
            acc[i] = x if acc[i] is None else acc[i] + x

        for t in range(dates):
            kvol, kgeo = kernel_of(t, r)
            weight = weight_of(flags[t, r, lanes])
            wvol = weight * kvol
            wgeo = weight * kgeo
            for i, x in enumerate((weight, wvol, wgeo, wvol * kvol, wvol * kgeo, wgeo * kgeo)):
                add(i, x)
            for b in range(bands):
                x = refl[t, b, r, lanes]
                add(6 + b, weight * x)
                add(6 + bands + b, wvol * x)
                add(6 + 2 * bands + b, wgeo * x)
        for i, x in enumerate(acc):
            sums[part, i, r] = x


def copies_in(sources, held, sems):
    dates = held[0].shape[0]
    for k in (1, 2, 3, 4, 0):
        for t in range(dates):
            pltpu.make_async_copy(sources[k].at[t], held[k].at[t], sems.at[k, t]).start()

    def wait(k, t):
        pltpu.make_async_copy(sources[k].at[t], held[k].at[t], sems.at[k, t]).wait()

    return wait


def far_kernel(*refs):
    sources, sums, kernels, held, sems = refs[:5], refs[5:7], refs[7], refs[8:13], refs[13]
    refl, sun, view, azim, flags = held
    dates, _, rows, cols = refl.shape
    ring = cols // LANES // 2
    wait = copies_in(sources, held, sems)
    blocks = [sums_part(3, flip, ring) for flip in (True, False)]
    for t in range(dates):
        for k in (1, 2, 3):
            wait(k, t)
        for block in blocks:
            lanes = lanes_of(block)
            for g in range(rows // SUB):
                r = slice(g * SUB, (g + 1) * SUB)
                kvol, kgeo = ross_li(sun[t, r, lanes], view[t, r, lanes], azim[t, r, lanes])
                kernels[block, t, 0, r] = kvol
                kernels[block, t, 1, r] = kgeo
    for k in (4, 0):
        for t in range(dates):
            wait(k, t)
    for block, total in zip(blocks, sums):
        kernel_of = lambda t, r: (kernels[block, t, 0, r], kernels[block, t, 1, r])
        add_dates(total, 0, block, refl, flags, kernel_of)


def rest_kernel(flip, refl, sun, view, azim, flags, _, sums, kernels):
    ring = refl.shape[3] // LANES // 2

    def one(i, carry):
        block = sums_part(i, flip, ring)
        lanes = lanes_of(block)

        def kernel_of(t, r):
            kvol, kgeo = ross_li(sun[t, r, lanes], view[t, r, lanes], azim[t, r, lanes])
            kernels[block, t, 0, r] = kvol
            kernels[block, t, 1, r] = kgeo
            return kvol, kgeo

        add_dates(sums, i, block, refl, flags, kernel_of)
        return carry

    lax.fori_loop(0, ring - 1, one, 0)


def sums_shape(refl, parts):
    _, bands, rows, _ = refl.shape
    return jax.ShapeDtypeStruct((parts, 6 + 3 * bands, rows, LANES), jnp.float32)


def kernels_shape(refl):
    dates, _, rows, cols = refl.shape
    return jax.ShapeDtypeStruct((cols // LANES, dates, 2, rows, LANES), jnp.float32)


def far_sums(*inputs):
    refl = inputs[0]
    held = [jax.ShapeDtypeStruct(x.shape, x.dtype) for x in inputs]
    return pl.pallas_call(
        far_kernel,
        in_specs=[pl.BlockSpec(memory_space=pltpu.HBM)] * 5,
        out_specs=[VMEM] * 8,
        out_shape=[sums_shape(refl, 1), sums_shape(refl, 1), kernels_shape(refl)] + held,
        scratch_shapes=[pltpu.SemaphoreType.DMA((5, refl.shape[0]))],
        compiler_params=pltpu.CompilerParams(vmem_limit_bytes=16 << 20),
        name="far_sums",
    )(*(pltpu.with_memory_space_constraint(x, pltpu.HBM) for x in inputs))


def rest_sums(flip, inputs, kernels):
    refl = inputs[0]
    ring = refl.shape[3] // LANES // 2
    return pl.pallas_call(
        functools.partial(rest_kernel, flip),
        in_specs=[VMEM] * 6,
        out_specs=[VMEM] * 2,
        out_shape=[sums_shape(refl, ring - 1), kernels_shape(refl)],
        input_output_aliases={5: 1},
        compiler_params=pltpu.CompilerParams(vmem_limit_bytes=16 << 20),
    )(*inputs, kernels)


def solve_kernel(own_a, own_b, near, far, smooth):
    planes, rows = smooth.shape[0] - 2, smooth.shape[1]
    bands = planes // 3
    groups = rows // SUB
    for g in range(groups):
        r = slice(g * SUB, (g + 1) * SUB)

        def total(i):
            return (own_a[0, i, r] + own_b[0, i, r]) + (near[i, r] + far[i, r])

        n00 = total(0) + ridge_weight
        n01 = total(1)
        n02 = total(2)
        n11 = total(3) + ridge_weight
        n12 = total(4)
        n22 = total(5) + ridge_weight
        c00 = n11 * n22 - n12 * n12
        c01 = n02 * n12 - n01 * n22
        c02 = n01 * n12 - n02 * n11
        c11 = n00 * n22 - n02 * n02
        c12 = n01 * n02 - n00 * n12
        c22 = n00 * n11 - n01 * n01
        inv_det = 1.0 / (n00 * c00 + n01 * c01 + n02 * c02)
        for b in range(bands):
            x, y, z = total(6 + b), total(6 + bands + b), total(6 + 2 * bands + b)
            smooth[b, r] = (c00 * x + c01 * y + c02 * z) * inv_det
            smooth[bands + b, r] = (c01 * x + c11 * y + c12 * z) * inv_det
            smooth[2 * bands + b, r] = (c02 * x + c12 * y + c22 * z) * inv_det
    row = lax.broadcasted_iota(jnp.int32, (SUB, LANES), 0)
    first, last = row == 0, row == SUB - 1
    zero = jnp.zeros((SUB, LANES), jnp.float32)
    smooth[planes:] = jnp.zeros((2,) + smooth.shape[1:], jnp.float32)
    up = ring_place()[1] == 0
    for p in range(planes):
        x = [smooth[p, g * SUB : (g + 1) * SUB] for g in range(groups)]
        low, high = x[0][:1] * 0.0625, x[-1][SUB - 1 :] * 0.0625
        smooth[planes, p : p + 1] = jnp.where(up, high, low)
        smooth[planes + 1, p : p + 1] = jnp.where(up, low, high)
        for g in range(groups):
            prior = jnp.where(last, x[g - 1] if g else zero, x[g])
            later = jnp.where(first, x[g + 1] if g < groups - 1 else zero, x[g])
            y = (pltpu.roll(prior, 1, 0) + 2.0 * x[g] + pltpu.roll(later, SUB - 1, 0)) * 0.0625
            smooth[p, g * SUB : (g + 1) * SUB] = y


def solve(own_a, own_b, near, far, bands):
    rows = own_a.shape[2]
    return pl.pallas_call(
        solve_kernel,
        in_specs=[VMEM] * 4,
        out_specs=VMEM,
        out_shape=jax.ShapeDtypeStruct((3 * bands + 2, rows, LANES), jnp.float32),
        compiler_params=pltpu.CompilerParams(vmem_limit_bytes=16 << 20),
        name="solve",
    )(own_a, own_b, near, far)


def correct_kernel(refl, kernels, nadir, *rest):
    (halo, *ends, beyond), pieces, (out, strip) = rest[:4], rest[4:-2], rest[-2:]
    step = pl.program_id(0)
    parts = pl.num_programs(0)
    dates, bands, rows, _ = out.shape
    planes, ring = 3 * bands, parts // 2

    @pl.when(step == 0)
    def _():
        strip[0] = jnp.zeros(strip.shape[1:], jnp.float32)
        strip[parts + 1] = jnp.zeros(strip.shape[1:], jnp.float32)
        place, core, way = ring_place()
        for (by, flip), piece, (source, at, sent_by) in zip(
            (
                (0, 0), (-way, 0), (-way, 1), (-2 * way, 0),
                (0, 1), (way, 1), (way, 0), (2 * way, 1),
            ),
            pieces,
            (
                (halo, (0, 3), core), (ends[0], (0, 3), core),
                (ends[0], (1, 2), core), (beyond, (0, 3), core),
                (halo, (1, 2), core), (ends[1], (0, 3), 1 - core),
                (ends[1], (1, 2), 1 - core), (beyond, (1, 2), core),
            ),
        ):
            spot = part_at(place + by, 1 - core if flip else core, ring) + 1
            top = jnp.where(sent_by == 0, at[0], at[1])
            bottom = jnp.where(sent_by == 0, at[1], at[0])
            for p in range(planes):
                strip[spot, p] = piece[p]
                strip[spot, p, :1] += source[top, p : p + 1]
                strip[spot, p, rows - 1 :] += source[bottom, p : p + 1]

    lanes = lanes_of(step)
    lane = lax.broadcasted_iota(jnp.int32, (SUB, LANES), 1)
    first, last = lane == 0, lane == LANES - 1
    for g in range(rows // SUB):
        r = slice(g * SUB, (g + 1) * SUB)
        kvol_n, kgeo_n = ross_li_nadir(nadir[r, lanes])

        def smooth(p):
            x = strip[step + 1, p, r]
            prior = pltpu.roll(jnp.where(last, strip[step, p, r], x), 1, 1)
            later = pltpu.roll(jnp.where(first, strip[step + 2, p, r], x), LANES - 1, 1)
            return prior + 2.0 * x + later

        for b in range(bands):
            iso, vol, geo = smooth(b), smooth(bands + b), smooth(2 * bands + b)
            model_n = iso + vol * kvol_n + geo * kgeo_n
            for t in range(dates):
                model = iso + vol * kernels[step, t, 0, r] + geo * kernels[step, t, 1, r]
                out[t, b, r] = refl[t, b, r, lanes] * model_n / jnp.maximum(model, model_floor)


def correct(refl, kernels, nadir, halos, pieces):
    dates, bands, rows, cols = refl.shape
    parts = cols // LANES
    return pl.pallas_call(
        correct_kernel,
        grid=(parts,),
        in_specs=[VMEM] * (3 + len(halos) + len(pieces)),
        out_specs=pl.BlockSpec((dates, bands, rows, LANES), lambda i: (0, 0, 0, i)),
        scratch_shapes=[pltpu.VMEM((parts + 2, 3 * bands, rows, LANES), jnp.float32)],
        out_shape=jax.ShapeDtypeStruct(refl.shape, jnp.float32),
        compiler_params=pltpu.CompilerParams(vmem_limit_bytes=24 << 20),
        name="correct",
    )(refl, kernels, nadir, *halos, *pieces)


def per_device(reflectance, sun_zenith, view_zenith, rel_azimuth, flags, nadir_sun):
    devices = lax.axis_size("dates")
    bands = reflectance.shape[1]

    def onward(x):
        pairs = [(i, (i + 2 - 4 * (i % 2)) % devices) for i in range(devices)]
        return lax.ppermute(x, "dates", pairs)

    def swap(x):
        return lax.ppermute(x, "dates", [(i, i ^ 1) for i in range(devices)])

    inputs = (reflectance, sun_zenith, view_zenith, rel_azimuth, flags)
    far_other, far_mine, kernels, *held = far_sums(*inputs)
    far_other = swap(far_other)
    other, kernels = rest_sums(True, held, kernels)
    other = swap(other)
    far = onward((far_mine + far_other)[0])
    mine, kernels = rest_sums(False, held, kernels)
    near = onward(mine[2] + other[2])
    far = onward(mine[1] + other[1] + far)
    near = swap(near)
    planes = 3 * bands
    own = solve(mine, other, near, far, bands)

    behind = onward(own[:planes])
    partner = swap(own)
    behind_partner = onward(partner[:planes])
    blocks = lax.axis_size("rows")
    pairs = []
    for r in range(blocks):
        for d in range(devices):
            to = r + 1 - 2 * (d % 2)
            if 0 <= to < blocks:
                pairs.append((r * devices + d, to * devices + d))
    edges = jnp.concatenate([own[planes : planes + 1], partner[planes + 1 :]], 0)
    edges = lax.ppermute(edges, ("rows", "dates"), pairs)
    halo = jnp.concatenate([edges, swap(edges)], 0)
    relayed = onward(behind)
    halo_behind = onward(halo)
    halo_far = lax.ppermute(
        halo, "dates", [(i, (i + devices // 2) % devices) for i in range(devices)]
    )
    pieces = (own, behind, behind_partner, relayed, partner)
    pieces += (swap(behind), swap(behind_partner), swap(relayed))
    halos = (halo, halo_behind, swap(halo_behind), halo_far)
    return correct(held[0], kernels, nadir_sun, halos, pieces)


def solution(mesh):
    in_specs = (
        P("dates", None, "rows", None),
        P("dates", "rows", None),
        P("dates", "rows", None),
        P("dates", "rows", None),
        P("dates", "rows", None),
        P("rows", None),
    )
    out_specs = P("dates", None, "rows", None)

    return jax.shard_map(
        per_device, mesh=mesh, in_specs=in_specs, out_specs=out_specs, check_vma=False
    )
```

```python
import functools
import math

import jax
import jax.numpy as jnp
from jax import lax
from jax.experimental import pallas as pl
from jax.experimental.pallas import tpu as pltpu
from jax.sharding import PartitionSpec as P

ridge_weight = 0.5
model_floor = 0.35
LANES = 128
SUB = 8
VMEM = pl.BlockSpec(memory_space=pltpu.VMEM)


SIN_SUN = (1.0, -0.1666666643, 0.008333314069, -0.0001983586641, 2.693759761e-06)
COS_SUN = (1.0, -0.4999999999, 0.04166666582, -0.001388885292, 2.479463838e-05, -2.693749222e-07)
SIN_VIEW = (1.0, -0.1666664847, 0.008321317392)
COS_VIEW = (1.0, -0.4999987263, 0.04158257081)
SIN_HALF = (1.0, -0.1666666662, 0.008333330977, -0.0001984086155, 2.752528678e-06, -2.388949223e-08)
GEO_POLY = (
    1.570796328, -1.214602072, -0.4109448018, 0.07413550608, -0.02841817795,
    0.01338202682, -0.005993092577, 0.001966222815, -0.0003219403671,
)
VOL_POLY = (
    0.999999995, -1.070795655, 0.08958698627, -0.02642109245, 0.01117480515,
    -0.004945099414, 0.001698688062, -0.0002986314728,
)


def poly(x, coefs):
    total = jnp.full_like(x, coefs[-1])
    for c in coefs[-2::-1]:
        total = total * x + c
    return total


def sin_cos_sun(sun):
    sq = sun * sun
    return sun * poly(sq, SIN_SUN), poly(sq, COS_SUN)


def shadow_term(cos_shadow):
    return jnp.sqrt(1.0 - cos_shadow) * poly(cos_shadow, GEO_POLY)


def ross_li(sun, view, azim):
    sin_s, cos_s = sin_cos_sun(sun)
    view_sq = view * view
    sin_v = view * poly(view_sq, SIN_VIEW)
    cos_v = poly(view_sq, COS_VIEW)
    half = 0.5 * azim
    sin_h = half * poly(half * half, SIN_HALF)
    half_sq = sin_h * sin_h
    cos_a = 1.0 - 2.0 * half_sq
    sin_a_sq = 4.0 * half_sq * (1.0 - half_sq)
    cos_cos = cos_s * cos_v
    sin_sin = sin_s * sin_v
    cos_phase = jnp.clip(cos_cos + sin_sin * cos_a, -1.0, 1.0)
    cos_sum = cos_s + cos_v
    inv = 1.0 / (cos_cos * cos_sum)
    sec_sec = cos_sum * inv
    inv_sum = cos_cos * inv
    kvol = (
        (0.5 * math.pi) * cos_phase + jnp.sqrt(1.0 - cos_phase) * poly(cos_phase, VOL_POLY)
    ) * inv_sum - 0.25 * math.pi
    tan_s = sin_s * cos_v
    tan_v = sin_v * cos_s
    dist_sq = jnp.maximum(tan_s * tan_s + tan_v * tan_v - 2.0 * tan_s * tan_v * cos_a, 0.0)
    cross_sq = sin_sin * sin_sin * sin_a_sq
    cos_shadow = jnp.clip(2.0 * jnp.sqrt(dist_sq + cross_sq) * inv_sum, -1.0, 1.0)
    kgeo = sec_sec * (
        cos_sum * (shadow_term(cos_shadow) * (1.0 / math.pi) - 1.0) + 0.5 * (1.0 + cos_phase)
    )
    return kvol, kgeo


def ross_li_nadir(sun):
    sin_s, cos_s = sin_cos_sun(sun)
    cos_sum = cos_s + 1.0
    inv = 1.0 / (cos_s * cos_sum)
    sec_s = cos_sum * inv
    inv_sum = cos_s * inv
    kvol = ((0.5 * math.pi - sun) * cos_s + sin_s) * inv_sum - 0.25 * math.pi
    cos_shadow = jnp.clip(2.0 * sin_s * inv_sum, -1.0, 1.0)
    kgeo = sec_s * (
        cos_sum * (shadow_term(cos_shadow) * (1.0 / math.pi) - 1.0) + 0.5 * (1.0 + cos_s)
    )
    return kvol, kgeo


def ring_place():
    index = lax.axis_index("dates")
    core = lax.rem(index, 2)
    return lax.div(index, 2), core, 1 - 2 * core


def part_at(place, core, ring):
    return core * ring + lax.rem(place + 2 * ring, ring)


def sums_part(i, flip, ring):
    place, core, way = ring_place()
    if flip:
        core, way = 1 - core, -way
    by = jnp.where(i == 0, 0, jnp.where(i == 3, 2, way))
    return part_at(place + by, jnp.where(i == 2, 1 - core, core), ring)


def lanes_of(part):
    return pl.ds(pl.multiple_of(part * LANES, LANES), LANES)


def weight_of(f):
    weight = jnp.where(f == 1, 0.3, jnp.where(f == 2, 0.7, jnp.where(f == 3, 1.0, 0.0)))
    return weight.astype(jnp.float32)


def add_dates(sums, part, block, refl, flags, kernel_of):
    dates, bands, rows, _ = refl.shape
    lanes = lanes_of(block)
    for g in range(rows // SUB):
        r = slice(g * SUB, (g + 1) * SUB)
        acc = [None] * (6 + 3 * bands)

        def add(i, x):
            acc[i] = x if acc[i] is None else acc[i] + x

        for t in range(dates):
            kvol, kgeo = kernel_of(t, r)
            weight = weight_of(flags[t, r, lanes])
            wvol = weight * kvol
            wgeo = weight * kgeo
            for i, x in enumerate((weight, wvol, wgeo, wvol * kvol, wvol * kgeo, wgeo * kgeo)):
                add(i, x)
            for b in range(bands):
                x = refl[t, b, r, lanes]
                add(6 + b, weight * x)
                add(6 + bands + b, wvol * x)
                add(6 + 2 * bands + b, wgeo * x)
        for i, x in enumerate(acc):
            sums[part, i, r] = x


def copies_in(sources, held, sems):
    dates = held[0].shape[0]
    for k in (1, 2, 3, 4, 0):
        for t in range(dates):
            pltpu.make_async_copy(sources[k].at[t], held[k].at[t], sems.at[k, t]).start()

    def wait(k, t):
        pltpu.make_async_copy(sources[k].at[t], held[k].at[t], sems.at[k, t]).wait()

    return wait


def far_kernel(*refs):
    sources, sums, kernels, held, sems = refs[:5], refs[5:7], refs[7], refs[8:13], refs[13]
    refl, sun, view, azim, flags = held
    dates, _, rows, cols = refl.shape
    ring = cols // LANES // 2
    wait = copies_in(sources, held, sems)
    blocks = [sums_part(3, flip, ring) for flip in (True, False)]
    for t in range(dates):
        for k in (1, 2, 3):
            wait(k, t)
        for block in blocks:
            lanes = lanes_of(block)
            for g in range(rows // SUB):
                r = slice(g * SUB, (g + 1) * SUB)
                kvol, kgeo = ross_li(sun[t, r, lanes], view[t, r, lanes], azim[t, r, lanes])
                kernels[block, t, 0, r] = kvol
                kernels[block, t, 1, r] = kgeo
    for k in (4, 0):
        for t in range(dates):
            wait(k, t)
    for block, total in zip(blocks, sums):
        kernel_of = lambda t, r: (kernels[block, t, 0, r], kernels[block, t, 1, r])
        add_dates(total, 0, block, refl, flags, kernel_of)


def rest_kernel(flip, refl, sun, view, azim, flags, _, sums, kernels):
    ring = refl.shape[3] // LANES // 2

    def one(i, carry):
        block = sums_part(i, flip, ring)
        lanes = lanes_of(block)

        def kernel_of(t, r):
            kvol, kgeo = ross_li(sun[t, r, lanes], view[t, r, lanes], azim[t, r, lanes])
            kernels[block, t, 0, r] = kvol
            kernels[block, t, 1, r] = kgeo
            return kvol, kgeo

        add_dates(sums, i, block, refl, flags, kernel_of)
        return carry

    lax.fori_loop(0, ring - 1, one, 0)


def sums_shape(refl, parts):
    _, bands, rows, _ = refl.shape
    return jax.ShapeDtypeStruct((parts, 6 + 3 * bands, rows, LANES), jnp.float32)


def kernels_shape(refl):
    dates, _, rows, cols = refl.shape
    return jax.ShapeDtypeStruct((cols // LANES, dates, 2, rows, LANES), jnp.float32)


def far_sums(*inputs):
    refl = inputs[0]
    held = [jax.ShapeDtypeStruct(x.shape, x.dtype) for x in inputs]
    return pl.pallas_call(
        far_kernel,
        in_specs=[pl.BlockSpec(memory_space=pltpu.HBM)] * 5,
        out_specs=[VMEM] * 8,
        out_shape=[sums_shape(refl, 1), sums_shape(refl, 1), kernels_shape(refl)] + held,
        scratch_shapes=[pltpu.SemaphoreType.DMA((5, refl.shape[0]))],
        compiler_params=pltpu.CompilerParams(vmem_limit_bytes=16 << 20),
        name="far_sums",
    )(*(pltpu.with_memory_space_constraint(x, pltpu.HBM) for x in inputs))


def rest_sums(flip, inputs, kernels):
    refl = inputs[0]
    ring = refl.shape[3] // LANES // 2
    return pl.pallas_call(
        functools.partial(rest_kernel, flip),
        in_specs=[VMEM] * 6,
        out_specs=[VMEM] * 2,
        out_shape=[sums_shape(refl, ring - 1), kernels_shape(refl)],
        input_output_aliases={5: 1},
        compiler_params=pltpu.CompilerParams(vmem_limit_bytes=16 << 20),
    )(*inputs, kernels)


def solve_kernel(own_a, own_b, near, far, smooth):
    planes, rows = smooth.shape[0] - 2, smooth.shape[1]
    bands = planes // 3
    groups = rows // SUB
    for g in range(groups):
        r = slice(g * SUB, (g + 1) * SUB)

        def total(i):
            return (own_a[0, i, r] + own_b[0, i, r]) + (near[i, r] + far[i, r])

        n00 = total(0) + ridge_weight
        n01 = total(1)
        n02 = total(2)
        n11 = total(3) + ridge_weight
        n12 = total(4)
        n22 = total(5) + ridge_weight
        c00 = n11 * n22 - n12 * n12
        c01 = n02 * n12 - n01 * n22
        c02 = n01 * n12 - n02 * n11
        c11 = n00 * n22 - n02 * n02
        c12 = n01 * n02 - n00 * n12
        c22 = n00 * n11 - n01 * n01
        inv_det = 1.0 / (n00 * c00 + n01 * c01 + n02 * c02)
        for b in range(bands):
            x, y, z = total(6 + b), total(6 + bands + b), total(6 + 2 * bands + b)
            smooth[b, r] = (c00 * x + c01 * y + c02 * z) * inv_det
            smooth[bands + b, r] = (c01 * x + c11 * y + c12 * z) * inv_det
            smooth[2 * bands + b, r] = (c02 * x + c12 * y + c22 * z) * inv_det
    row = lax.broadcasted_iota(jnp.int32, (SUB, LANES), 0)
    first, last = row == 0, row == SUB - 1
    zero = jnp.zeros((SUB, LANES), jnp.float32)
    smooth[planes:] = jnp.zeros((2,) + smooth.shape[1:], jnp.float32)
    up = ring_place()[1] == 0
    for p in range(planes):
        x = [smooth[p, g * SUB : (g + 1) * SUB] for g in range(groups)]
        low, high = x[0][:1] * 0.0625, x[-1][SUB - 1 :] * 0.0625
        smooth[planes, p : p + 1] = jnp.where(up, high, low)
        smooth[planes + 1, p : p + 1] = jnp.where(up, low, high)
        for g in range(groups):
            prior = jnp.where(last, x[g - 1] if g else zero, x[g])
            later = jnp.where(first, x[g + 1] if g < groups - 1 else zero, x[g])
            y = (pltpu.roll(prior, 1, 0) + 2.0 * x[g] + pltpu.roll(later, SUB - 1, 0)) * 0.0625
            smooth[p, g * SUB : (g + 1) * SUB] = y


def solve(own_a, own_b, near, far, bands):
    rows = own_a.shape[2]
    return pl.pallas_call(
        solve_kernel,
        in_specs=[VMEM] * 4,
        out_specs=VMEM,
        out_shape=jax.ShapeDtypeStruct((3 * bands + 2, rows, LANES), jnp.float32),
        compiler_params=pltpu.CompilerParams(vmem_limit_bytes=16 << 20),
        name="solve",
    )(own_a, own_b, near, far)


def correct_kernel(refl, kernels, nadir, *rest):
    (halo, beyond), pieces, (out, strip) = rest[:2], rest[2:-2], rest[-2:]
    step = pl.program_id(0)
    parts = pl.num_programs(0)
    dates, bands, rows, _ = out.shape
    planes, ring = 3 * bands, parts // 2

    @pl.when(step == 0)
    def _():
        strip[0] = jnp.zeros(strip.shape[1:], jnp.float32)
        strip[parts + 1] = jnp.zeros(strip.shape[1:], jnp.float32)
        place, core, way = ring_place()
        ends = (pieces[3], pieces[7])
        for (by, flip), piece, (source, at, sent_by) in zip(
            (
                (0, 0), (-way, 0), (-way, 1), (-2 * way, 0),
                (0, 1), (way, 1), (way, 0), (2 * way, 1),
            ),
            pieces,
            (
                (halo, (0, 3), core), (ends[0], (planes, planes + 3), core),
                (ends[0], (planes + 1, planes + 2), core), (beyond, (0, 3), core),
                (halo, (1, 2), core), (ends[1], (planes, planes + 3), 1 - core),
                (ends[1], (planes + 1, planes + 2), 1 - core), (beyond, (1, 2), core),
            ),
        ):
            spot = part_at(place + by, 1 - core if flip else core, ring) + 1
            top = jnp.where(sent_by == 0, at[0], at[1])
            bottom = jnp.where(sent_by == 0, at[1], at[0])
            for p in range(planes):
                strip[spot, p] = piece[p]
                strip[spot, p, :1] += source[top, p : p + 1]
                strip[spot, p, rows - 1 :] += source[bottom, p : p + 1]

    lanes = lanes_of(step)
    lane = lax.broadcasted_iota(jnp.int32, (SUB, LANES), 1)
    first, last = lane == 0, lane == LANES - 1
    for g in range(rows // SUB):
        r = slice(g * SUB, (g + 1) * SUB)
        kvol_n, kgeo_n = ross_li_nadir(nadir[r, lanes])

        def smooth(p):
            x = strip[step + 1, p, r]
            prior = pltpu.roll(jnp.where(last, strip[step, p, r], x), 1, 1)
            later = pltpu.roll(jnp.where(first, strip[step + 2, p, r], x), LANES - 1, 1)
            return prior + 2.0 * x + later

        for b in range(bands):
            iso, vol, geo = smooth(b), smooth(bands + b), smooth(2 * bands + b)
            model_n = iso + vol * kvol_n + geo * kgeo_n
            for t in range(dates):
                model = iso + vol * kernels[step, t, 0, r] + geo * kernels[step, t, 1, r]
                out[t, b, r] = refl[t, b, r, lanes] * model_n / jnp.maximum(model, model_floor)


def correct(refl, kernels, nadir, halos, pieces):
    dates, bands, rows, cols = refl.shape
    parts = cols // LANES
    return pl.pallas_call(
        correct_kernel,
        grid=(parts,),
        in_specs=[VMEM] * (3 + len(halos) + len(pieces)),
        out_specs=pl.BlockSpec((dates, bands, rows, LANES), lambda i: (0, 0, 0, i)),
        scratch_shapes=[pltpu.VMEM((parts + 2, 3 * bands, rows, LANES), jnp.float32)],
        out_shape=jax.ShapeDtypeStruct(refl.shape, jnp.float32),
        compiler_params=pltpu.CompilerParams(vmem_limit_bytes=24 << 20),
        name="correct",
    )(refl, kernels, nadir, *halos, *pieces)


def per_device(reflectance, sun_zenith, view_zenith, rel_azimuth, flags, nadir_sun):
    devices = lax.axis_size("dates")
    bands = reflectance.shape[1]

    def onward(x):
        pairs = [(i, (i + 2 - 4 * (i % 2)) % devices) for i in range(devices)]
        return lax.ppermute(x, "dates", pairs)

    def swap(x):
        return lax.ppermute(x, "dates", [(i, i ^ 1) for i in range(devices)])

    inputs = (reflectance, sun_zenith, view_zenith, rel_azimuth, flags)
    far_other, far_mine, kernels, *held = far_sums(*inputs)
    far_other = swap(far_other)
    other, kernels = rest_sums(True, held, kernels)
    other = swap(other)
    far = onward((far_mine + far_other)[0])
    mine, kernels = rest_sums(False, held, kernels)
    near = onward(mine[2] + other[2])
    far = onward(mine[1] + other[1] + far)
    near = swap(near)
    planes = 3 * bands
    own = solve(mine, other, near, far, bands)

    behind = onward(own[:planes])
    partner = swap(own)
    behind_partner = onward(partner[:planes])
    blocks = lax.axis_size("rows")
    pairs = []
    for r in range(blocks):
        for d in range(devices):
            to = r + 1 - 2 * (d % 2)
            if 0 <= to < blocks:
                pairs.append((r * devices + d, to * devices + d))
    edges = jnp.concatenate([own[planes : planes + 1], partner[planes + 1 :]], 0)
    edges = lax.ppermute(edges, ("rows", "dates"), pairs)
    halo = jnp.concatenate([edges, swap(edges)], 0)
    relayed = onward(jnp.concatenate([behind, halo], 0))
    halo_far = lax.ppermute(
        halo, "dates", [(i, (i + devices // 2) % devices) for i in range(devices)]
    )
    pieces = (own, behind, behind_partner, relayed, partner)
    pieces += (swap(behind), swap(behind_partner), swap(relayed))
    return correct(held[0], kernels, nadir_sun, (halo, halo_far), pieces)


def solution(mesh):
    in_specs = (
        P("dates", None, "rows", None),
        P("dates", "rows", None),
        P("dates", "rows", None),
        P("dates", "rows", None),
        P("dates", "rows", None),
        P("rows", None),
    )
    out_specs = P("dates", None, "rows", None)

    return jax.shard_map(
        per_device, mesh=mesh, in_specs=in_specs, out_specs=out_specs, check_vma=False
    )
```
